32 devices in a mesh: rep: 8 (over z, x), grp: 4 (over y, core).
Axes of the slice: x: 2, y: 2, z: 4, core: 2. Of those that a mesh axis runs over, the one named last changes fastest.
Arguments:
- hidden: bfloat16 [8192, 768], P(('rep', 'grp')), may hold values from -6 to 6
- prev_logits: bfloat16 [12, 8192, 1024], P(None, ('rep', 'grp')), may hold values from -6 to 6
- prefix: int32 [8], replicated, may hold values from 102 to 512
- w_query: bfloat16 [768, 768], P('grp'), may hold values from -0.21875 to 0.21875
- w_key: bfloat16 [768, 768], P('grp'), may hold values from -0.21875 to 0.21875
- w_value: bfloat16 [768, 768], P('grp'), may hold values from -0.21875 to 0.21875
- w_output: bfloat16 [768, 768], P('grp'), may hold values from -3.5 to 3.5
- w_inner: bfloat16 [768, 3072], P('grp'), may hold values from -0.21875 to 0.21875
- w_outer: bfloat16 [3072, 768], P('grp'), may hold values from -0.109375 to 0.109375
- b_query: bfloat16 [768], P('grp'), may hold values from -2 to 2
- b_value: bfloat16 [768], P('grp'), may hold values from -2 to 2
- b_output: bfloat16 [768], P('grp'), may hold values from -2 to 2
- b_inner: bfloat16 [3072], P('grp'), may hold values from -2 to 2
- b_outer: bfloat16 [768], P('grp'), may hold values from -2 to 2
- gain_attn: bfloat16 [768], P('grp'), may hold values from 0.5 to 1.5
- shift_attn: bfloat16 [768], P('grp'), may hold values from -2 to 2
- gain_feed: bfloat16 [768], P('grp'), may hold values from 0.5 to 1.5
- shift_feed: bfloat16 [768], P('grp'), may hold values from -2 to 2
- out_grad: bfloat16 [8192, 768], P(('rep', 'grp')), may hold values from -6 to 6
- logit_grad: bfloat16 [12, 8192, 1024], P(None, ('rep', 'grp')), may hold values from -6 to 6
Outputs:
- output: bfloat16 [8192, 768], P(('rep', 'grp'))
- new_logits: bfloat16 [12, 8192, 1024], P(None, ('rep', 'grp'))
- grad_hidden: bfloat16 [8192, 768], P(('rep', 'grp'))
- grad_prev_logits: bfloat16 [12, 8192, 1024], P(None, ('rep', 'grp'))
- grad_w_query: float32 [768, 768], P('grp')
- grad_w_key: float32 [768, 768], P('grp')
- grad_w_value: float32 [768, 768], P('grp')
- grad_w_output: float32 [768, 768], P('grp')
- grad_w_inner: float32 [768, 3072], P('grp')
- grad_w_outer: float32 [3072, 768], P('grp')
- grad_b_query: float32 [768], P('grp')
- grad_b_value: float32 [768], P('grp')
- grad_b_output: float32 [768], P('grp')
- grad_b_inner: float32 [3072], P('grp')
- grad_b_outer: float32 [768], P('grp')
- grad_gain_attn: float32 [768], P('grp')
- grad_shift_attn: float32 [768], P('grp')
- grad_gain_feed: float32 [768], P('grp')
- grad_shift_feed: float32 [768], P('grp')
The draws below stay inside these ranges and needn't reach their ends.
Inputs may be any that keep to these rules, and one draw needn't show every extreme that they name: prefix[s] is the number of leading tokens of sequence s that every query of that sequence may attend.
All inputs are finite; a program needn't handle non-finite values.
Results may differ from the reference program's by a relative error of at most 0.017.
Values may be sent and summed in bfloat16 or wider, within the bound.
No kernel may reach another device: no remote copies, remote signals or barrier semaphores. Data moves between devices by JAX's collectives and lax.ppermute only.
A program may use at most 192 MiB of HBM per device.

```python
import jax
import jax.numpy as jnp
from jax import lax

D = 768
HEADS = 12
FF = 3072
LEN = 1024
SEQS = 8
TOKENS = 8192


def with_ends(drawn, stream_key, smallest, top_value):
    place = [jax.random.randint(jax.random.fold_in(stream_key, axis), (), 0, length) for axis, length in enumerate(drawn.shape)]
    longest = drawn.shape.index(max(drawn.shape))
    next_to = place[:longest] + [(place[longest] + 1) % drawn.shape[longest]] + place[longest + 1:]
    return drawn.at[tuple(place)].set(smallest).at[tuple(next_to)].set(top_value)


def level_of(own_key, dims, cuts, low, largest):
    def one(dim, shards_of):
        steps = jax.random.uniform(jax.random.fold_in(jax.random.fold_in(own_key, 6), dim), (shards_of,), jnp.float32, low / len(cuts), largest / len(cuts))
        return jnp.repeat(jnp.exp(steps), dims[dim] // shards_of).reshape((-1,) + (1,) * (len(dims) - dim - 1))

    factor_of = one(*cuts[0])
    for cut in cuts[1:]:
        factor_of = factor_of * one(*cut)
    return factor_of


def scatter_about(own_key, shape, scale, most, shards=(), held_as=jnp.bfloat16):
    drawn = jax.random.normal(own_key, shape, jnp.float32) * scale
    if len(shards) > 0:
        drawn = level_of(own_key, shape, shards, -0.22, 0.18) * drawn
    return jnp.clip(drawn, min=-most, max=most).astype(held_as)


def setup_inputs(seed: int = 0) -> dict:
    streams_of = jax.random.split(jax.random.key(seed), 21)
    hidden = scatter_about(streams_of[0], (TOKENS, D), 1.0, 6.0, ((0, 32),))
    prev_logits = scatter_about(streams_of[1], (HEADS, TOKENS, LEN), 1.0, 6.0, ((1, 32),))
    prefix = with_ends(jax.random.randint(streams_of[2], (SEQS,), LEN // 10, LEN // 2 + 1), jax.random.fold_in(streams_of[2], 1), LEN // 10, (LEN // 2 + 1) - 1).astype(jnp.int32)
    w_query = scatter_about(streams_of[3], (D, D), D ** -0.5, 0.21875, ((0, 4),))
    w_key = scatter_about(streams_of[4], (D, D), D ** -0.5, 0.21875, ((0, 4),))
    w_value = scatter_about(streams_of[5], (D, D), D ** -0.5, 0.21875, ((0, 4),))
    w_output = scatter_about(streams_of[6], (D, D), (max(D // 256, 1)) ** -0.5, 3.5, ((0, 4),))
    w_inner = scatter_about(streams_of[7], (D, FF), D ** -0.5, 0.21875, ((0, 4),))
    w_outer = scatter_about(streams_of[8], (FF, D), FF ** -0.5, 0.109375, ((0, 4),))
    b_query = scatter_about(streams_of[9], (D,), 0.3, 2.0, ((0, 4),))
    b_value = scatter_about(streams_of[10], (D,), 0.3, 2.0, ((0, 4),))
    b_output = scatter_about(streams_of[11], (D,), 0.3, 2.0, ((0, 4),))
    b_inner = scatter_about(streams_of[12], (FF,), 0.3, 2.0, ((0, 4),))
    b_outer = scatter_about(streams_of[13], (D,), 0.3, 2.0, ((0, 4),))
    gain_attn = jnp.clip(1.0 + 0.1 * jax.random.normal(streams_of[14], (D,), jnp.float32), 0.5, 1.5).astype(jnp.bfloat16)
    shift_attn = scatter_about(streams_of[15], (D,), 0.3, 2.0, ((0, 4),))
    gain_feed = jnp.clip(1.0 + 0.1 * jax.random.normal(streams_of[16], (D,), jnp.float32), 0.5, 1.5).astype(jnp.bfloat16)
    shift_feed = scatter_about(streams_of[17], (D,), 0.3, 2.0, ((0, 4),))
    out_grad = scatter_about(streams_of[18], (TOKENS, D), 1.0, 6.0, ((0, 32),))
    logit_grad = scatter_about(streams_of[19], (HEADS, TOKENS, LEN), 1.0, 6.0, ((1, 32),))
    return dict(hidden=hidden, prev_logits=prev_logits, prefix=prefix, w_query=w_query, w_key=w_key, w_value=w_value, w_output=w_output, w_inner=w_inner, w_outer=w_outer, b_query=b_query, b_value=b_value, b_output=b_output, b_inner=b_inner, b_outer=b_outer, gain_attn=gain_attn, shift_attn=shift_attn, gain_feed=gain_feed, shift_feed=shift_feed, out_grad=out_grad, logit_grad=logit_grad)


@jax.custom_vjp
def low(v):
    return lax.optimization_barrier(v.astype(jnp.bfloat16)).astype(jnp.float32)

@jax.custom_vjp
def low_back(v):
    return v

def low_keep(v):
    return (low(v), None)

def low_pass(kept, grad):
    return (grad,)

def back_keep(v):
    return (v, None)

def back_low(kept, grad):
    return (low(grad),)
low.defvjp(low_keep, low_pass)
low_back.defvjp(back_keep, back_low)
epsilon = 1e-06

def layer_norm(values, gain, shift):
    center = values - lax.optimization_barrier(jnp.mean(values, axis=-1, keepdims=True))
    spread = lax.optimization_barrier(jnp.mean(center * center, axis=-1, keepdims=True))
    return center * lax.rsqrt(spread + epsilon) * gain + shift

def forward(tokens, logits_in, params, prefix_len):
    highest = lax.Precision.HIGHEST
    query_mat, key_mat, value_mat, output_mat, inner_mat, outer_mat, query_bias, value_bias, output_bias, inner_bias, outer_bias, attn_gain, attn_shift, feed_gain, feed_shift = params
    length = tokens.shape[0]
    head_dim = D // HEADS
    queries = low(low_back(jnp.dot(tokens, query_mat, precision=highest) + query_bias)).reshape(length, HEADS, head_dim)
    key_rows = low(low_back(jnp.dot(tokens, key_mat, precision=highest))).reshape(length, HEADS, head_dim)
    value_rows = low(low_back(jnp.dot(tokens, value_mat, precision=highest) + value_bias)).reshape(length, HEADS, head_dim)
    scores = jnp.einsum('qhe,khe->hqk', queries, key_rows, precision=highest) * 0.125 + logits_in
    scores = low_back(scores)
    positions = jnp.arange(length, dtype=jnp.int32)
    allowed = (positions[None, :] < prefix_len) | (positions[None, :] <= positions[:, None])
    masked = jnp.where(allowed[None], scores, -1e+30)
    row_top = lax.optimization_barrier(jnp.max(masked, axis=-1, keepdims=True))
    exp_terms = jnp.exp(masked - row_top)
    attn_probs = exp_terms / lax.optimization_barrier(jnp.sum(exp_terms, axis=-1, keepdims=True))
    context = jnp.einsum('hqk,khe->qhe', low(attn_probs), value_rows, precision=highest).reshape(length, D)
    context = low(low_back(context))
    attn_out = low_back(jnp.dot(context, output_mat, precision=highest) + output_bias)
    normed = low(layer_norm(tokens + attn_out, attn_gain, attn_shift))
    inner_act = low_back(jnp.dot(normed, inner_mat, precision=highest) + inner_bias)
    middle = low(jax.nn.gelu(inner_act))
    feed_out = low_back(jnp.dot(middle, outer_mat, precision=highest) + outer_bias)
    return (layer_norm(normed + feed_out, feed_gain, feed_shift), scores)

def add_pair(first, second):
    return first + second

def reference(hidden, prev_logits, prefix, w_query, w_key, w_value, w_output, w_inner, w_outer, b_query, b_value, b_output, b_inner, b_outer, gain_attn, shift_attn, gain_feed, shift_feed, out_grad, logit_grad):
    params = tuple((item.astype(jnp.float32) for item in (w_query, w_key, w_value, w_output, w_inner, w_outer, b_query, b_value, b_output, b_inner, b_outer, gain_attn, shift_attn, gain_feed, shift_feed)))

    def one_sequence(totals, items):
        tokens, logits_in, prefix_len, grad_out, grad_logits = items

        def local(tok_values, logit_values, param_values):
            return forward(tok_values, logit_values, param_values, prefix_len)
        (result, scores), pull = jax.vjp(jax.checkpoint(local), tokens.astype(jnp.float32), logits_in.astype(jnp.float32), params)
        grad_tokens, grad_in_logits, grad_params = pull((grad_out.astype(jnp.float32), grad_logits.astype(jnp.float32)))
        totals = jax.tree.map(add_pair, totals, grad_params)
        return (totals, (result.astype(jnp.bfloat16), scores.astype(jnp.bfloat16), grad_tokens.astype(jnp.bfloat16), grad_in_logits.astype(jnp.bfloat16)))
    logits_seq = prev_logits.reshape(HEADS, SEQS, LEN, LEN).transpose(1, 0, 2, 3)
    grads_seq = logit_grad.reshape(HEADS, SEQS, LEN, LEN).transpose(1, 0, 2, 3)
    zeros = tuple((jnp.zeros(item.shape, jnp.float32) for item in params))
    totals, results = lax.scan(one_sequence, zeros, (hidden.reshape(SEQS, LEN, D), logits_seq, prefix, out_grad.reshape(SEQS, LEN, D), grads_seq))
    new_logits = results[1].transpose(1, 0, 2, 3).reshape(HEADS, TOKENS, LEN)
    grad_logits_out = results[3].transpose(1, 0, 2, 3).reshape(HEADS, TOKENS, LEN)
    return (results[0].reshape(TOKENS, D), new_logits, results[2].reshape(TOKENS, D), grad_logits_out, totals[0], totals[1], totals[2], totals[3], totals[4], totals[5], totals[6], totals[7], totals[8], totals[9], totals[10], totals[11], totals[12], totals[13], totals[14])
```

```python
import jax
import jax.numpy as jnp
from jax import lax
from jax.sharding import PartitionSpec as P

HEADS = 12
epsilon = 1e-06
LOW = jnp.bfloat16
F32 = jnp.float32


def mat_dot(left, right):
    return jnp.dot(left, right, preferred_element_type=F32)


def left_dot(left, right):
    return lax.dot_general(left, right, (((0,), (0,)), ((), ())), preferred_element_type=F32)


def right_dot(left, right):
    return lax.dot_general(left, right, (((1,), (1,)), ((), ())), preferred_element_type=F32)


def layer_norm(values, gain, shift):
    center = values - jnp.mean(values, axis=-1, keepdims=True)
    spread = jnp.mean(center * center, axis=-1, keepdims=True)
    scale = lax.rsqrt(spread + epsilon)
    normed = center * scale
    return (normed * gain + shift, normed, scale)


def norm_back(grad_out, normed, scale, gain):
    grad_norm = grad_out * gain
    grad_in = scale * (
        grad_norm
        - jnp.mean(grad_norm, axis=-1, keepdims=True)
        - normed * jnp.mean(grad_norm * normed, axis=-1, keepdims=True)
    )
    return (grad_in, jnp.sum(grad_out * normed, axis=0), jnp.sum(grad_out, axis=0))


def make_body(rep_size, grp_size):
    def swap(value, axis, bit):
        size = rep_size if axis == "rep" else grp_size
        return lax.ppermute(value, axis, [(i, i ^ bit) for i in range(size)])

    def pick(value, index, axis=0):
        return lax.dynamic_index_in_dim(value, index, axis, keepdims=False)

    def place(mine, other, bit):
        both = jnp.zeros((2,) + mine.shape, mine.dtype)
        both = lax.dynamic_update_index_in_dim(both, mine, bit, 0)
        return lax.dynamic_update_index_in_dim(both, other, 1 - bit, 0)

    def gather_group(shard, group):
        far = swap(shard, "grp", 2)
        near = swap(shard, "grp", 1)
        diag = swap(far, "grp", 1)
        whole = jnp.zeros((4,) + shard.shape, shard.dtype)
        for step, piece in enumerate((shard, near, far, diag)):
            whole = lax.dynamic_update_index_in_dim(whole, piece, group ^ step, 0)
        return whole

    def rep_bits(rep):
        count = rep_size.bit_length() - 1
        return [(1 << k, (rep >> k) & 1) for k in range(count)]

    def halve(value, bits, extra=None):
        for step, bit in bits:
            split = value.reshape((2, value.shape[0] // 2) + value.shape[1:])
            sent, kept = (pick(split, 1 - bit), pick(split, bit))
            if extra is not None:
                sent = jnp.concatenate((sent, extra), axis=0)
            got = swap(sent, "rep", step)
            if extra is not None:
                rows = kept.shape[0]
                extra = (extra.astype(F32) + got[rows:].astype(F32)).astype(LOW)
                got = got[:rows]
            value = (kept.astype(F32) + got.astype(F32)).astype(LOW)
        return value, extra

    def double(value, bits):
        for step, bit in reversed(bits):
            other = swap(value, "rep", step)
            if step == 1:
                value, other = value.astype(F32), other.astype(F32)
            value = place(value, other, bit)
            value = value.reshape((value.shape[0] * value.shape[1],) + value.shape[2:])
        return value

    def core_stage(value, core, extra=None):
        sent, kept = (pick(value, 1 - core, 1), pick(value, core, 1))
        shape = sent.shape
        sent = sent.reshape((-1, shape[-1]))
        if extra is not None:
            sent = jnp.concatenate((sent, extra), axis=0)
        got = swap(sent, "grp", 1)
        rows = shape[0] * shape[1]
        if extra is not None:
            extra = (extra.astype(F32) + got[rows:].astype(F32)).astype(LOW)
            got = got[:rows]
        return (kept.astype(F32) + got.reshape(shape).astype(F32)).astype(LOW), extra

    def far_stage(value, far_bit, extra=None):
        sent, kept = (pick(value, 1 - far_bit), pick(value, far_bit))
        if extra is not None:
            sent = jnp.concatenate((sent, extra), axis=0)
        got = swap(sent, "grp", 2)
        rows = kept.shape[0]
        if extra is not None:
            extra = (extra.astype(F32) + got[rows:].astype(F32)).astype(LOW)
            got = got[:rows]
        return (kept.astype(F32) + got.astype(F32)).astype(LOW), extra

    def body(
        hidden,
        prev_logits,
        prefix,
        w_query,
        w_key,
        w_value,
        w_output,
        w_inner,
        w_outer,
        b_query,
        b_value,
        b_output,
        b_inner,
        b_outer,
        gain_attn,
        shift_attn,
        gain_feed,
        shift_feed,
        out_grad,
        logit_grad,
    ):
        rows, width = hidden.shape
        shard = w_query.shape[0]
        hidden_width = w_inner.shape[1]
        length = prev_logits.shape[2]
        head_dim = width // HEADS
        rep = lax.axis_index("rep")
        group = lax.axis_index("grp")
        core = group & 1
        far_bit = group >> 1
        bits = rep_bits(rep)
        vectors = (b_query, b_value, b_output, b_inner, b_outer, gain_attn, shift_attn, gain_feed, shift_feed)
        vec_sizes = [item.shape[0] for item in vectors]
        vec_rows = sum(vec_sizes) // width
        vec = jnp.concatenate(vectors).reshape(vec_rows, width)
        pad = jnp.zeros((16 - vec_rows, width), LOW)
        pack = jnp.concatenate((hidden, w_query, w_key, w_value, vec, pad), axis=0)
        pack_all = gather_group(pack, group)
        tokens_all = pack_all[:, :rows].reshape(length, width)
        query_mat, key_mat, value_mat = [
            pack_all[:, rows + k * shard : rows + (k + 1) * shard].reshape(width, width) for k in range(3)
        ]
        vec_all = pack_all[:, rows + 3 * shard : rows + 3 * shard + vec_rows].reshape(4, vec_rows * width)
        vec_all = vec_all.astype(F32)
        full_vectors = []
        offset = 0
        for size in vec_sizes:
            full_vectors.append(vec_all[:, offset : offset + size].reshape(4 * size))
            offset += size
        query_bias, value_bias, output_bias, inner_bias, outer_bias = full_vectors[:5]
        attn_gain, attn_shift, feed_gain, feed_shift = full_vectors[5:]
        output_mat = gather_group(w_output, group).reshape(width, width)
        inner_mat = gather_group(w_inner, group).reshape(width, hidden_width)
        outer_mat = gather_group(w_outer, group).reshape(hidden_width, width)

        queries = (mat_dot(hidden, query_mat) + query_bias).astype(LOW)
        group_keys = mat_dot(tokens_all, key_mat).astype(LOW)
        group_values = (mat_dot(tokens_all, value_mat) + value_bias).astype(LOW)
        query_heads = queries.reshape(rows, HEADS, head_dim)
        key_heads = group_keys.reshape(length, HEADS, head_dim)
        value_heads = group_values.reshape(length, HEADS, head_dim)
        scores = jnp.einsum("rhe,khe->hrk", query_heads, key_heads, preferred_element_type=F32) * 0.125
        scores = scores + prev_logits.astype(F32)
        row_start = group * rows
        query_pos = row_start + jnp.arange(rows, dtype=jnp.int32)[:, None]
        key_pos = jnp.arange(length, dtype=jnp.int32)[None, :]
        prefix_len = prefix[rep]
        allowed = (key_pos < prefix_len) | (key_pos <= query_pos)
        masked = jnp.where(allowed[None], scores, -1e30)
        row_top = jnp.max(masked, axis=-1, keepdims=True)
        exp_terms = jnp.exp(masked - row_top)
        attn_probs = exp_terms / jnp.sum(exp_terms, axis=-1, keepdims=True)
        probs_low = attn_probs.astype(LOW)
        context = jnp.einsum("hrk,khe->rhe", probs_low, value_heads, preferred_element_type=F32)
        context = context.reshape(rows, width).astype(LOW)
        attn_out = mat_dot(context, output_mat) + output_bias
        first_out, first_norm, first_scale = layer_norm(hidden.astype(F32) + attn_out, attn_gain, attn_shift)
        first_low = first_out.astype(LOW)
        inner_act = mat_dot(first_low, inner_mat) + inner_bias
        gelu_out, gelu_pull = jax.vjp(jax.nn.gelu, inner_act)
        middle = gelu_out.astype(LOW)
        feed_out = mat_dot(middle, outer_mat) + outer_bias
        output, second_norm, second_scale = layer_norm(first_low.astype(F32) + feed_out, feed_gain, feed_shift)
        grad_second, grad_gfeed, grad_sfeed = norm_back(
            out_grad.astype(F32), second_norm, second_scale, feed_gain
        )
        grad_feed = grad_second.astype(LOW)
        grad_bouter = jnp.sum(grad_feed.astype(F32), axis=0)
        grad_wouter = left_dot(middle, grad_feed).astype(LOW).reshape(2, 2, -1, width)
        outer_part, _ = core_stage(grad_wouter, core)
        outer_part, _ = far_stage(outer_part, far_bit)
        outer_part, _ = halve(outer_part, bits)
        outer_total = double(outer_part, bits)
        grad_middle = right_dot(grad_feed, outer_mat)
        grad_inner = gelu_pull(grad_middle)[0].astype(LOW)
        grad_binner = jnp.sum(grad_inner.astype(F32), axis=0)
        grad_winner = left_dot(first_low, grad_inner).astype(LOW).reshape(2, 2, shard, hidden_width)
        inner_part, _ = core_stage(grad_winner, core)
        inner_part, _ = far_stage(inner_part, far_bit)
        inner_part, _ = halve(inner_part, bits)
        inner_total = double(inner_part, bits)
        grad_first = grad_second + right_dot(grad_inner, inner_mat)
        grad_resid, grad_gattn, grad_sattn = norm_back(grad_first, first_norm, first_scale, attn_gain)
        grad_attn = grad_resid.astype(LOW)
        grad_boutput = jnp.sum(grad_attn.astype(F32), axis=0)
        grad_woutput = left_dot(context, grad_attn)
        grad_context = right_dot(grad_attn, output_mat).astype(LOW).reshape(rows, HEADS, head_dim)
        grad_probs = jnp.einsum("rhe,khe->hrk", grad_context, value_heads, preferred_element_type=F32)
        grad_values = jnp.einsum("hrk,rhe->khe", probs_low, grad_context, preferred_element_type=F32)
        grad_scores = attn_probs * (grad_probs - jnp.sum(grad_probs * attn_probs, axis=-1, keepdims=True))
        grad_scores = (grad_scores + logit_grad.astype(F32)).astype(LOW)
        grad_queries = jnp.einsum("hrk,khe->rhe", grad_scores, key_heads, preferred_element_type=F32) * 0.125
        grad_queries = grad_queries.astype(LOW).reshape(rows, width)
        grad_keys = jnp.einsum("hrk,rhe->khe", grad_scores, query_heads, preferred_element_type=F32) * 0.125
        grad_keys = grad_keys.astype(LOW).reshape(length, width)
        grad_values = grad_values.astype(LOW).reshape(length, width)
        grad_bquery = jnp.sum(grad_queries.astype(F32), axis=0)
        grad_bvalue = jnp.sum(grad_values.astype(F32), axis=0)
        grad_wquery = left_dot(hidden, grad_queries)
        grad_wkey = left_dot(tokens_all, grad_keys)
        grad_wvalue = left_dot(tokens_all, grad_values)
        grad_own = grad_resid + right_dot(grad_queries, query_mat)
        grad_rows = (right_dot(grad_keys, key_mat) + right_dot(grad_values, value_mat)).astype(LOW)

        vec_grads = (
            grad_bquery,
            grad_bvalue,
            grad_boutput,
            grad_binner,
            grad_bouter,
            grad_gattn,
            grad_sattn,
            grad_gfeed,
            grad_sfeed,
        )
        vec_pack = jnp.concatenate([item.reshape(4, -1) for item in vec_grads], axis=1).astype(LOW)
        vec_pack = vec_pack.reshape(4 * vec_rows, width)
        vec_pack = jnp.concatenate((vec_pack, jnp.zeros((16 - 4 * vec_rows, width), LOW)), axis=0)
        attn_pack = jnp.concatenate(
            [
                item.astype(LOW).reshape(2, 2, -1, width)
                for item in (grad_wquery, grad_wkey, grad_wvalue, grad_woutput, grad_rows)
            ],
            axis=2,
        )
        attn_part, vec_pack = core_stage(attn_pack, core, vec_pack)
        attn_part, vec_pack = far_stage(attn_part, far_bit, vec_pack)
        grad_input = grad_own + attn_part[4 * shard :].astype(F32)
        attn_part, vec_pack = halve(attn_part[: 4 * shard], bits, vec_pack)
        attn_total = double(attn_part, bits)
        vec_own = pick(vec_pack[: 4 * vec_rows].reshape(4, vec_rows * width), group).astype(F32)
        vec_outs = []
        offset = 0
        for size in vec_sizes:
            vec_outs.append(vec_own[offset : offset + size])
            offset += size
        return (
            output.astype(LOW),
            scores.astype(LOW),
            grad_input.astype(LOW),
            grad_scores,
            attn_total[:shard],
            attn_total[shard : 2 * shard],
            attn_total[2 * shard : 3 * shard],
            attn_total[3 * shard :],
            inner_total,
            outer_total,
            *vec_outs,
        )

    return body


def solution(mesh):
    rows = P(("rep", "grp"), None)
    logits = P(None, ("rep", "grp"), None)
    matrix = P("grp", None)
    vector = P("grp")
    return jax.shard_map(
        make_body(mesh.shape["rep"], mesh.shape["grp"]),
        mesh=mesh,
        in_specs=(rows, logits, P(), *(matrix,) * 6, *(vector,) * 9, rows, logits),
        out_specs=(rows, logits, rows, logits, *(matrix,) * 6, *(vector,) * 9),
        check_vma=False,
    )
```

```python
import jax
import jax.numpy as jnp
from jax import lax
from jax.experimental import pallas as pl
from jax.experimental.pallas import tpu as pltpu
from jax.sharding import PartitionSpec as P

HEADS = 12
epsilon = 1e-06
LOW = jnp.bfloat16
F32 = jnp.float32
ANY = pl.BlockSpec(memory_space=pl.ANY)


def mat_dot(left, right):
    return jnp.dot(left, right, preferred_element_type=F32)


def left_dot(left, right):
    return lax.dot_general(left, right, (((0,), (0,)), ((), ())), preferred_element_type=F32)


def right_dot(left, right):
    return lax.dot_general(left, right, (((1,), (1,)), ((), ())), preferred_element_type=F32)


def layer_norm(values, gain, shift):
    center = values - jnp.mean(values, axis=-1, keepdims=True)
    spread = jnp.mean(center * center, axis=-1, keepdims=True)
    scale = lax.rsqrt(spread + epsilon)
    normed = center * scale
    return (normed * gain + shift, normed, scale)


def norm_back(grad_out, normed, scale, gain):
    grad_norm = grad_out * gain
    grad_in = scale * (
        grad_norm
        - jnp.mean(grad_norm, axis=-1, keepdims=True)
        - normed * jnp.mean(grad_norm * normed, axis=-1, keepdims=True)
    )
    return (grad_in, jnp.sum(grad_out * normed, axis=0), jnp.sum(grad_out, axis=0))


def run_copies(copies, sems):
    started = [pltpu.make_async_copy(a, b, sems.at[i]) for i, (a, b) in enumerate(copies)]
    for copy in started:
        copy.start()
    for copy in started:
        copy.wait()


def pack_rows(parts):
    counts = [part.shape[0] for part in parts]
    width = parts[0].shape[1]

    def kernel(*refs):
        ins, out, sems = refs[: len(parts)], refs[-2], refs[-1]
        copies = []
        start = 0
        for ref, count in zip(ins, counts):
            copies.append((ref, out.at[pl.ds(start, count)]))
            start += count
        run_copies(copies, sems)

    return pl.pallas_call(
        kernel,
        out_shape=jax.ShapeDtypeStruct((sum(counts), width), parts[0].dtype),
        in_specs=[ANY] * len(parts),
        out_specs=ANY,
        scratch_shapes=[pltpu.SemaphoreType.DMA((len(parts),))],
    )(*parts)


def assemble(pieces, counts):
    width = pieces[0].shape[1]
    align = 64

    def kernel(*refs):
        ins, outs, sems = refs[:4], refs[4:-1], refs[-1]
        me = lax.axis_index("grp")
        copies = []
        for step, ref in enumerate(ins):
            owner = me ^ step
            start = 0
            for out, count in zip(outs, counts):
                place = pl.multiple_of(owner * count, align)
                copies.append((ref.at[pl.ds(start, count)], out.at[pl.ds(place, count)]))
                start += count
        run_copies(copies, sems)

    return pl.pallas_call(
        kernel,
        out_shape=[jax.ShapeDtypeStruct((4 * count, width), pieces[0].dtype) for count in counts],
        in_specs=[ANY] * 4,
        out_specs=[ANY] * len(counts),
        scratch_shapes=[pltpu.SemaphoreType.DMA((4 * len(counts),))],
    )(*pieces)


def split_by_core(parts):
    counts = [part.shape[2] for part in parts]
    width = parts[0].shape[3]

    def kernel(*refs):
        ins, sent, kept, sems = refs[: len(parts)], refs[-3], refs[-2], refs[-1]
        core = lax.axis_index("grp") & 1
        copies = []
        for out, owner in ((sent, 1 - core), (kept, core)):
            start = 0
            for ref, count in zip(ins, counts):
                for far in range(2):
                    copies.append((ref.at[far, owner], out.at[far, pl.ds(start, count)]))
                start += count
        run_copies(copies, sems)

    shape = jax.ShapeDtypeStruct((2, sum(counts), width), parts[0].dtype)
    return pl.pallas_call(
        kernel,
        out_shape=[shape, shape],
        in_specs=[ANY] * len(parts),
        out_specs=[ANY, ANY],
        scratch_shapes=[pltpu.SemaphoreType.DMA((4 * len(parts),))],
    )(*parts)


def nt_dot(left, right):
    return lax.dot_general(left, right, (((1,), (1,)), ((), ())), preferred_element_type=F32)


def nn_dot(left, right):
    return lax.dot_general(left, right, (((1,), (0,)), ((), ())), preferred_element_type=F32)


def attend(place, queries, keys, values, prev_logits):
    rows, width = queries.shape
    length = keys.shape[0]
    head_dim = width // HEADS
    each = 128 // head_dim
    cols = each * head_dim

    def kernel(place_ref, q_ref, k_ref, v_ref, prev_ref, new_ref, prob_ref, ctx_ref):
        lane = lax.broadcasted_iota(jnp.int32, (rows, cols), 1)
        key_pos = lax.broadcasted_iota(jnp.int32, (rows, length), 1)
        query_pos = place_ref[1] + lax.broadcasted_iota(jnp.int32, (rows, length), 0)
        allowed = (key_pos < place_ref[0]) | (key_pos <= query_pos)
        q = q_ref[...].astype(F32) * 0.125
        k = k_ref[...]
        v = v_ref[...]
        context = jnp.zeros((rows, cols), F32)
        for h in range(each):
            mine = (lane >= h * head_dim) & (lane < (h + 1) * head_dim)
            scores = nt_dot(jnp.where(mine, q, 0.0).astype(LOW), k) + prev_ref[h].astype(F32)
            new_ref[h] = scores.astype(LOW)
            scores = jnp.where(allowed, scores, -1e30)
            terms = jnp.exp(scores - jnp.max(scores, axis=-1, keepdims=True))
            probs = (terms * (1.0 / jnp.sum(terms, axis=-1, keepdims=True))).astype(LOW)
            prob_ref[h] = probs
            context = jnp.where(mine, nn_dot(probs, v), context)
        ctx_ref[...] = context.astype(LOW)

    tall = pl.BlockSpec((length, cols), lambda i: (0, i))
    wide = pl.BlockSpec((rows, cols), lambda i: (0, i))
    square = pl.BlockSpec((each, rows, length), lambda i: (i, 0, 0))
    squares = jax.ShapeDtypeStruct((HEADS, rows, length), LOW)
    return pl.pallas_call(
        kernel,
        grid=(HEADS // each,),
        out_shape=[squares, squares, jax.ShapeDtypeStruct((rows, width), LOW)],
        in_specs=[pl.BlockSpec(memory_space=pltpu.SMEM), wide, tall, tall, square],
        out_specs=[square, square, wide],
    )(place, queries, keys, values, prev_logits)


def attend_back(queries, keys, values, probs, logit_grad, grad_context):
    rows, width = queries.shape
    length = keys.shape[0]
    head_dim = width // HEADS
    each = 128 // head_dim
    cols = each * head_dim

    def kernel(q_ref, k_ref, v_ref, prob_ref, lg_ref, dc_ref, ds_ref, dq_ref, dk_ref, dv_ref):
        lane = lax.broadcasted_iota(jnp.int32, (rows, cols), 1)
        dc = dc_ref[...].astype(F32)
        dc_turned = dc.T.astype(LOW)
        q_turned = (q_ref[...].astype(F32) * 0.125).T.astype(LOW)
        k = k_ref[...]
        v = v_ref[...]
        dq = jnp.zeros((rows, cols), F32)
        dk, dv = [], []
        for h in range(each):
            own = slice(h * head_dim, (h + 1) * head_dim)
            mine = (lane >= h * head_dim) & (lane < (h + 1) * head_dim)
            prob_low = prob_ref[h]
            prob = prob_low.astype(F32)
            dp = nt_dot(jnp.where(mine, dc, 0.0).astype(LOW), v)
            ds = prob * (dp - jnp.sum(dp * prob, axis=-1, keepdims=True)) + lg_ref[h].astype(F32)
            ds = ds.astype(LOW)
            ds_ref[h] = ds
            dq = jnp.where(mine, nn_dot(ds, k), dq)
            dv.append(nn_dot(dc_turned[own], prob_low))
            dk.append(nn_dot(q_turned[own], ds))
        dq_ref[...] = (dq * 0.125).astype(LOW)
        dk_ref[...] = jnp.concatenate(dk, axis=0).T.astype(LOW)
        dv_ref[...] = jnp.concatenate(dv, axis=0).T.astype(LOW)

    tall = pl.BlockSpec((length, cols), lambda i: (0, i))
    wide = pl.BlockSpec((rows, cols), lambda i: (0, i))
    square = pl.BlockSpec((each, rows, length), lambda i: (i, 0, 0))
    talls = jax.ShapeDtypeStruct((length, width), LOW)
    return pl.pallas_call(
        kernel,
        grid=(HEADS // each,),
        out_shape=[jax.ShapeDtypeStruct((HEADS, rows, length), LOW), jax.ShapeDtypeStruct((rows, width), LOW), talls, talls],
        in_specs=[wide, tall, tall, square, square, wide],
        out_specs=[square, wide, tall, tall],
    )(queries, keys, values, probs, logit_grad, grad_context)


def make_body(rep_size, grp_size):
    def swap(value, axis, bit):
        size = rep_size if axis == "rep" else grp_size
        return lax.ppermute(value, axis, [(i, i ^ bit) for i in range(size)])

    def pick(value, index, axis=0):
        return lax.dynamic_index_in_dim(value, index, axis, keepdims=False)

    def place(mine, other, bit):
        both = jnp.zeros((2,) + mine.shape, mine.dtype)
        both = lax.dynamic_update_index_in_dim(both, mine, bit, 0)
        return lax.dynamic_update_index_in_dim(both, other, 1 - bit, 0)

    def gather_group(shard):
        far = swap(shard, "grp", 2)
        near = swap(shard, "grp", 1)
        diag = swap(far, "grp", 1)
        return shard, near, far, diag

    def rep_bits(rep):
        count = rep_size.bit_length() - 1
        return [(1 << k, (rep >> k) & 1) for k in range(count)]

    def summed(parts):
        total = parts[0].astype(F32)
        for part in parts[1:]:
            total = total + part.astype(F32)
        return total

    def shrink(parts, axis, step, bit):
        sent = summed([pick(part, 1 - bit) for part in parts]).astype(LOW)
        kept = summed([pick(part, bit) for part in parts]).astype(LOW)
        return [kept, swap(sent, axis, step)]

    def in_two(part):
        return part.reshape((2, part.shape[0] // 2) + part.shape[1:])

    def reduce_rep(parts, bits):
        for step, bit in bits:
            parts = shrink([in_two(part) for part in parts], "rep", step, bit)
        value = summed(parts).astype(LOW)
        for step, bit in reversed(bits[1:]):
            other = swap(value, "rep", step)
            value = place(value, other, bit)
            value = value.reshape((value.shape[0] * value.shape[1],) + value.shape[2:])
        step, bit = bits[0]
        return value, swap(value, "rep", step)

    def finish(pair, bits):
        mine, other = pair
        value = place(mine.astype(F32), other.astype(F32), bits[0][1])
        return value.reshape((value.shape[0] * value.shape[1],) + value.shape[2:])

    def inner_body(
        hidden,
        prev_logits,
        prefix,
        w_query,
        w_key,
        w_value,
        w_output,
        w_inner,
        w_outer,
        b_query,
        b_value,
        b_output,
        b_inner,
        b_outer,
        gain_attn,
        shift_attn,
        gain_feed,
        shift_feed,
        out_grad,
        logit_grad,
    ):
        rows, width = hidden.shape
        shard = w_query.shape[0]
        feed_shard = w_outer.shape[0]
        rep = lax.axis_index("rep")
        group = lax.axis_index("grp")
        core = group & 1
        far_bit = group >> 1
        bits = rep_bits(rep)
        pack = pack_rows((hidden, w_query, w_key, w_value))
        pack_pieces = gather_group(pack)
        vectors = (b_query, b_value, b_output, b_inner, b_outer, gain_attn, shift_attn, gain_feed, shift_feed)
        vec_sizes = [item.shape[0] for item in vectors]
        vec_count = sum(vec_sizes)
        vec = jnp.concatenate(vectors)
        vec_pieces = gather_group(vec)
        output_pieces = gather_group(w_output)
        inner_pieces = gather_group(w_inner)
        outer_pieces = gather_group(w_outer)

        vec_all = jnp.zeros((4, vec_count), F32)
        for step, piece in enumerate(vec_pieces):
            vec_all = lax.dynamic_update_index_in_dim(vec_all, piece.astype(F32), group ^ step, 0)
        full_vectors = []
        offset = 0
        for size in vec_sizes:
            full_vectors.append(vec_all[:, offset : offset + size].reshape(4 * size))
            offset += size
        query_bias, value_bias, output_bias, inner_bias, outer_bias = full_vectors[:5]
        attn_gain, attn_shift, feed_gain, feed_shift = full_vectors[5:]

        tokens_all, query_mat, key_mat, value_mat = assemble(pack_pieces, (rows, shard, shard, shard))
        queries = (mat_dot(hidden, query_mat) + query_bias).astype(LOW)
        group_keys = mat_dot(tokens_all, key_mat).astype(LOW)
        group_values = (mat_dot(tokens_all, value_mat) + value_bias).astype(LOW)
        position = jnp.stack([prefix[rep], (group * rows).astype(jnp.int32)])
        new_logits, probs, context = attend(position, queries, group_keys, group_values, prev_logits)
        (output_mat,) = assemble(output_pieces, (shard,))
        (inner_mat,) = assemble(inner_pieces, (shard,))
        (outer_mat,) = assemble(outer_pieces, (feed_shard,))

        attn_out = mat_dot(context, output_mat) + output_bias
        first_out, first_norm, first_scale = layer_norm(hidden.astype(F32) + attn_out, attn_gain, attn_shift)
        first_low = first_out.astype(LOW)
        inner_act = mat_dot(first_low, inner_mat) + inner_bias
        gelu_out, gelu_pull = jax.vjp(jax.nn.gelu, inner_act)
        middle, slope = lax.optimization_barrier((gelu_out.astype(LOW), gelu_pull(jnp.ones_like(inner_act))[0]))
        feed_out = mat_dot(middle, outer_mat) + outer_bias
        output, second_norm, second_scale = layer_norm(first_low.astype(F32) + feed_out, feed_gain, feed_shift)
        grad_second, grad_gfeed, grad_sfeed = norm_back(
            out_grad.astype(F32), second_norm, second_scale, feed_gain
        )
        grad_feed = lax.optimization_barrier(grad_second.astype(LOW))
        grad_bouter = jnp.sum(grad_feed.astype(F32), axis=0)

        def reduce_group(value):
            split = value.astype(LOW).reshape((2, 2, -1) + value.shape[1:])
            sent, kept = pick(split, 1 - core, 1), pick(split, core, 1)
            parts = [kept, swap(sent, "grp", 1)]
            return shrink(parts, "grp", 2, far_bit)

        grad_wouter = left_dot(middle, grad_feed)
        outer_pair = reduce_rep(reduce_group(grad_wouter), bits)
        grad_inner = (right_dot(grad_feed, outer_mat) * slope).astype(LOW)
        grad_inner = lax.optimization_barrier(grad_inner)
        grad_binner = jnp.sum(grad_inner.astype(F32), axis=0)
        grad_winner = left_dot(first_low, grad_inner)
        inner_pair = reduce_rep(reduce_group(grad_winner), bits)
        grad_first = grad_second + right_dot(grad_inner, inner_mat)
        grad_resid, grad_gattn, grad_sattn = norm_back(grad_first, first_norm, first_scale, attn_gain)
        grad_attn = lax.optimization_barrier(grad_resid.astype(LOW))
        grad_boutput = jnp.sum(grad_attn.astype(F32), axis=0)
        grad_context = right_dot(grad_attn, output_mat).astype(LOW)
        grad_scores, grad_queries, grad_keys, grad_values = attend_back(
            queries, group_keys, group_values, probs, logit_grad, grad_context
        )
        grad_bquery = jnp.sum(grad_queries.astype(F32), axis=0)
        grad_bvalue = jnp.sum(grad_values.astype(F32), axis=0)
        grad_woutput = left_dot(context, grad_attn)
        grad_wquery = left_dot(hidden, grad_queries)
        grad_wkey = left_dot(tokens_all, grad_keys)
        grad_wvalue = left_dot(tokens_all, grad_values)
        grad_own = grad_resid + right_dot(grad_queries, query_mat)
        grad_rows = (right_dot(grad_keys, key_mat) + right_dot(grad_values, value_mat)).astype(LOW)

        vec_grads = (
            grad_bquery,
            grad_bvalue,
            grad_boutput,
            grad_binner,
            grad_bouter,
            grad_gattn,
            grad_sattn,
            grad_gfeed,
            grad_sfeed,
        )
        vec_sum = jnp.concatenate([item.reshape(4, -1) for item in vec_grads], axis=1)
        vec_sum = vec_sum + swap(vec_sum, "grp", 1)
        vec_sum = pick(vec_sum.reshape(2, 2, vec_count), core, 1)
        vec_sum = pick(vec_sum, far_bit) + swap(pick(vec_sum, 1 - far_bit), "grp", 2)
        for step, _ in bits:
            vec_sum = vec_sum + swap(vec_sum, "rep", step)

        sent, kept = split_by_core(
            [
                item.astype(LOW).reshape(2, 2, -1, width)
                for item in (grad_wquery, grad_wkey, grad_wvalue, grad_woutput, grad_rows)
            ]
        )
        attn_parts = [kept, swap(sent, "grp", 1)]
        attn_parts = shrink(attn_parts, "grp", 2, far_bit)
        grad_input = grad_own + summed([part[4 * shard :] for part in attn_parts])
        mine, other = reduce_rep([part[: 4 * shard] for part in attn_parts], bits)
        low_bit = bits[0][1]
        attn_grads = []
        for k in range(4):
            cut = slice((k % 2) * shard, (k % 2 + 1) * shard)
            attn_grads.append(jnp.where(low_bit == k // 2, mine[cut], other[cut]).astype(F32))
        vec_outs = []
        offset = 0
        for size in vec_sizes:
            vec_outs.append(vec_sum[offset : offset + size])
            offset += size
        return (
            output.astype(LOW),
            new_logits,
            grad_input.astype(LOW),
            grad_scores,
            *attn_grads,
            finish(inner_pair, bits),
            finish(outer_pair, bits),
            *vec_outs,
        )

    return inner_body


def solution(mesh):
    rows = P(("rep", "grp"), None)
    logits = P(None, ("rep", "grp"), None)
    matrix = P("grp", None)
    vector = P("grp")
    return jax.shard_map(
        make_body(mesh.shape["rep"], mesh.shape["grp"]),
        mesh=mesh,
        in_specs=(rows, logits, P(), *(matrix,) * 6, *(vector,) * 9, rows, logits),
        out_specs=(rows, logits, rows, logits, *(matrix,) * 6, *(vector,) * 9),
        check_vma=False,
    )
```

```python
import jax
import jax.numpy as jnp
from jax import lax
from jax.experimental import pallas as pl
from jax.experimental.pallas import tpu as pltpu
from jax.sharding import PartitionSpec as P


HEADS = 12
epsilon = 1e-06
LOW = jnp.bfloat16
F32 = jnp.float32
ANY = pl.BlockSpec(memory_space=pl.ANY)
INSIDE = pl.BlockSpec(memory_space=pltpu.VMEM)


def mat_dot(left, right):
    return jnp.dot(left, right, preferred_element_type=F32)


def left_dot(left, right):
    return lax.dot_general(left, right, (((0,), (0,)), ((), ())), preferred_element_type=F32)


def right_dot(left, right):
    return lax.dot_general(left, right, (((1,), (1,)), ((), ())), preferred_element_type=F32)


def layer_norm(values, gain, shift):
    center = values - jnp.mean(values, axis=-1, keepdims=True)
    spread = jnp.mean(center * center, axis=-1, keepdims=True)
    scale = lax.rsqrt(spread + epsilon)
    normed = center * scale
    return (normed * gain + shift, normed, scale)


def norm_back(grad_out, normed, scale, gain):
    grad_norm = grad_out * gain
    grad_in = scale * (
        grad_norm
        - jnp.mean(grad_norm, axis=-1, keepdims=True)
        - normed * jnp.mean(grad_norm * normed, axis=-1, keepdims=True)
    )
    return (grad_in, jnp.sum(grad_out * normed, axis=0), jnp.sum(grad_out, axis=0))


def run_copies(copies, sems):
    started = [pltpu.make_async_copy(a, b, sems.at[i]) for i, (a, b) in enumerate(copies)]
    for copy in started:
        copy.start()
    for copy in started:
        copy.wait()


def pack_rows(parts):
    counts = [part.shape[0] for part in parts]
    width = parts[0].shape[1]

    def kernel(*refs):
        ins, out, sems = refs[: len(parts)], refs[-2], refs[-1]
        copies = []
        start = 0
        for ref, count in zip(ins, counts):
            copies.append((ref, out.at[pl.ds(start, count)]))
            start += count
        run_copies(copies, sems)

    return pl.pallas_call(
        kernel,
        out_shape=jax.ShapeDtypeStruct((sum(counts), width), parts[0].dtype),
        in_specs=[ANY] * len(parts),
        out_specs=INSIDE,
        scratch_shapes=[pltpu.SemaphoreType.DMA((len(parts),))],
    )(*parts)


def assemble(pieces, counts):
    arrays = [piece[0] for piece in pieces]
    width = arrays[0].shape[1]

    def kernel(*refs):
        ins, outs, sems = refs[: len(arrays)], refs[len(arrays) : -1], refs[-1]
        me = lax.axis_index("grp")
        low = lax.axis_index("rep") & 1
        copies = []
        for ref, (_, step, half) in zip(ins, pieces):
            start = 0
            for out, count in zip(outs, counts):
                rows = count if half is None else count // 2
                at = (me ^ step) * count
                if half is not None:
                    at = at + (low ^ half) * rows
                copies.append((ref.at[pl.ds(start, rows)], out.at[pl.ds(pl.multiple_of(at, 32), rows)]))
                start += rows
        run_copies(copies, sems)

    return pl.pallas_call(
        kernel,
        out_shape=[jax.ShapeDtypeStruct((4 * count, width), arrays[0].dtype) for count in counts],
        in_specs=[ANY] * len(arrays),
        out_specs=[INSIDE] * len(counts),
        scratch_shapes=[pltpu.SemaphoreType.DMA((len(arrays) * len(counts),))],
    )(*arrays)


def split_by_core(parts):
    counts = [part.shape[2] for part in parts]
    width = parts[0].shape[3]

    def kernel(*refs):
        ins, sent, kept, sems = refs[: len(parts)], refs[-3], refs[-2], refs[-1]
        core = lax.axis_index("grp") & 1
        copies = []
        for out, owner in ((sent, 1 - core), (kept, core)):
            start = 0
            for ref, count in zip(ins, counts):
                for far in range(2):
                    copies.append((ref.at[far, owner], out.at[far, pl.ds(start, count)]))
                start += count
        run_copies(copies, sems)

    shape = jax.ShapeDtypeStruct((2, sum(counts), width), parts[0].dtype)
    return pl.pallas_call(
        kernel,
        out_shape=[shape, shape],
        in_specs=[ANY] * len(parts),
        out_specs=[INSIDE, INSIDE],
        scratch_shapes=[pltpu.SemaphoreType.DMA((4 * len(parts),))],
    )(*parts)


def nt_dot(left, right):
    return lax.dot_general(left, right, (((1,), (1,)), ((), ())), preferred_element_type=F32)


def nn_dot(left, right):
    return lax.dot_general(left, right, (((1,), (0,)), ((), ())), preferred_element_type=F32)


def attend(place, queries, keys, values, prev_logits):
    rows, width = queries.shape
    length = keys.shape[0]
    head_dim = width // HEADS
    each = 128 // head_dim
    cols = each * head_dim

    def kernel(place_ref, q_ref, k_ref, v_ref, prev_ref, new_ref, prob_ref, ctx_ref):
        lane = lax.broadcasted_iota(jnp.int32, (rows, cols), 1)
        key_pos = lax.broadcasted_iota(jnp.int32, (rows, length), 1)
        query_pos = place_ref[1] + lax.broadcasted_iota(jnp.int32, (rows, length), 0)
        allowed = (key_pos < place_ref[0]) | (key_pos <= query_pos)
        q = q_ref[...].astype(F32) * 0.125
        k = k_ref[...]
        v = v_ref[...]
        context = jnp.zeros((rows, cols), F32)
        for h in range(each):
            mine = (lane >= h * head_dim) & (lane < (h + 1) * head_dim)
            scores = nt_dot(jnp.where(mine, q, 0.0).astype(LOW), k) + prev_ref[h].astype(F32)
            new_ref[h] = scores.astype(LOW)
            scores = jnp.where(allowed, scores, -1e30)
            terms = jnp.exp(scores - jnp.max(scores, axis=-1, keepdims=True))
            probs = (terms * (1.0 / jnp.sum(terms, axis=-1, keepdims=True))).astype(LOW)
            prob_ref[h] = probs
            context = jnp.where(mine, nn_dot(probs, v), context)
        ctx_ref[...] = context.astype(LOW)

    tall = pl.BlockSpec((length, cols), lambda i: (0, i))
    wide = pl.BlockSpec((rows, cols), lambda i: (0, i))
    square = pl.BlockSpec((each, rows, length), lambda i: (i, 0, 0))
    squares = jax.ShapeDtypeStruct((HEADS, rows, length), LOW)
    return pl.pallas_call(
        kernel,
        grid=(HEADS // each,),
        out_shape=[squares, squares, jax.ShapeDtypeStruct((rows, width), LOW)],
        in_specs=[pl.BlockSpec(memory_space=pltpu.SMEM), wide, tall, tall, square],
        out_specs=[square, square, wide],
    )(place, queries, keys, values, prev_logits)


def attend_back(queries, keys, values, probs, logit_grad, grad_context):
    rows, width = queries.shape
    length = keys.shape[0]
    head_dim = width // HEADS
    each = 128 // head_dim
    cols = each * head_dim

    def kernel(q_ref, k_ref, v_ref, prob_ref, lg_ref, dc_ref, ds_ref, dq_ref, dk_ref, dv_ref):
        lane = lax.broadcasted_iota(jnp.int32, (rows, cols), 1)
        dc = dc_ref[...].astype(F32)
        dc_turned = dc.T.astype(LOW)
        q_turned = (q_ref[...].astype(F32) * 0.125).T.astype(LOW)
        k = k_ref[...]
        v = v_ref[...]
        dq = jnp.zeros((rows, cols), F32)
        dk, dv = [], []
        for h in range(each):
            own = slice(h * head_dim, (h + 1) * head_dim)
            mine = (lane >= h * head_dim) & (lane < (h + 1) * head_dim)
            prob_low = prob_ref[h]
            prob = prob_low.astype(F32)
            dp = nt_dot(jnp.where(mine, dc, 0.0).astype(LOW), v)
            ds = prob * (dp - jnp.sum(dp * prob, axis=-1, keepdims=True)) + lg_ref[h].astype(F32)
            ds = ds.astype(LOW)
            ds_ref[h] = ds
            dq = jnp.where(mine, nn_dot(ds, k), dq)
            dv.append(nn_dot(dc_turned[own], prob_low))
            dk.append(nn_dot(q_turned[own], ds))
        dq_ref[...] = (dq * 0.125).astype(LOW)
        dk_ref[...] = jnp.concatenate(dk, axis=0).T.astype(LOW)
        dv_ref[...] = jnp.concatenate(dv, axis=0).T.astype(LOW)

    tall = pl.BlockSpec((length, cols), lambda i: (0, i))
    wide = pl.BlockSpec((rows, cols), lambda i: (0, i))
    square = pl.BlockSpec((each, rows, length), lambda i: (i, 0, 0))
    talls = jax.ShapeDtypeStruct((length, width), LOW)
    return pl.pallas_call(
        kernel,
        grid=(HEADS // each,),
        out_shape=[jax.ShapeDtypeStruct((HEADS, rows, length), LOW), jax.ShapeDtypeStruct((rows, width), LOW), talls, talls],
        in_specs=[wide, tall, tall, square, square, wide],
        out_specs=[square, wide, tall, tall],
    )(queries, keys, values, probs, logit_grad, grad_context)


def make_body(rep_size, grp_size):
    def swap(value, axis, bit):
        size = rep_size if axis == "rep" else grp_size
        return lax.ppermute(value, axis, [(i, i ^ bit) for i in range(size)])

    def pick(value, index, axis=0):
        return lax.dynamic_index_in_dim(value, index, axis, keepdims=False)

    def place(mine, other, bit):
        both = jnp.zeros((2,) + mine.shape, mine.dtype)
        both = lax.dynamic_update_index_in_dim(both, mine, bit, 0)
        return lax.dynamic_update_index_in_dim(both, other, 1 - bit, 0)

    def gather_group(shard):
        far = swap(shard, "grp", 2)
        near = swap(shard, "grp", 1)
        diag = swap(far, "grp", 1)
        return (shard, 0, None), (near, 1, None), (far, 2, None), (diag, 3, None)

    def gather_halves(shard, low):
        half = pick(in_two(shard), low)
        near = swap(shard, "grp", 1)
        far = swap(half, "grp", 2)
        side = swap(far, "rep", 1)
        diag = swap(far, "grp", 1)
        last = swap(side, "grp", 1)
        return (shard, 0, None), (near, 1, None), (far, 2, 0), (side, 2, 1), (diag, 3, 0), (last, 3, 1)

    def rep_bits(rep):
        count = rep_size.bit_length() - 1
        return [(1 << k, (rep >> k) & 1) for k in range(count)]

    def summed(parts):
        total = parts[0].astype(F32)
        for part in parts[1:]:
            total = total + part.astype(F32)
        return total

    def shrink(parts, axis, step, bit):
        sent = summed([pick(part, 1 - bit) for part in parts]).astype(LOW)
        kept = summed([pick(part, bit) for part in parts]).astype(LOW)
        return [kept, swap(sent, axis, step)]

    def in_two(part):
        return part.reshape((2, part.shape[0] // 2) + part.shape[1:])

    def reduce_rep(parts, bits):
        for step, bit in bits:
            parts = shrink([in_two(part) for part in parts], "rep", step, bit)
        value = summed(parts).astype(LOW)
        for step, bit in reversed(bits[1:]):
            other = swap(value, "rep", step)
            value = place(value, other, bit)
            value = value.reshape((value.shape[0] * value.shape[1],) + value.shape[2:])
        step, bit = bits[0]
        return value, swap(value, "rep", step)

    def finish(pair, bits):
        mine, other = pair
        value = place(mine.astype(F32), other.astype(F32), bits[0][1])
        return value.reshape((value.shape[0] * value.shape[1],) + value.shape[2:])

    def inner_body(
        hidden,
        prev_logits,
        prefix,
        w_query,
        w_key,
        w_value,
        w_output,
        w_inner,
        w_outer,
        b_query,
        b_value,
        b_output,
        b_inner,
        b_outer,
        gain_attn,
        shift_attn,
        gain_feed,
        shift_feed,
        out_grad,
        logit_grad,
    ):
        rows, width = hidden.shape
        shard = w_query.shape[0]
        feed_shard = w_outer.shape[0]
        rep = lax.axis_index("rep")
        group = lax.axis_index("grp")
        core = group & 1
        far_bit = group >> 1
        bits = rep_bits(rep)
        pack = pack_rows((hidden, w_query, w_key, w_value))
        pack_pieces = gather_group(pack)
        vectors = (b_query, b_value, b_output, b_inner, b_outer, gain_attn, shift_attn, gain_feed, shift_feed)
        vec_sizes = [item.shape[0] for item in vectors]
        vec_count = sum(vec_sizes)
        vec = jnp.concatenate(vectors)
        vec_pieces = gather_group(vec)
        output_pieces = gather_group(w_output)
        inner_pieces = gather_halves(w_inner, rep & 1)
        outer_pieces = gather_halves(w_outer, rep & 1)

        vec_all = jnp.zeros((4, vec_count), F32)
        for piece, step, _ in vec_pieces:
            vec_all = lax.dynamic_update_index_in_dim(vec_all, piece.astype(F32), group ^ step, 0)
        full_vectors = []
        offset = 0
        for size in vec_sizes:
            full_vectors.append(vec_all[:, offset : offset + size].reshape(4 * size))
            offset += size
        query_bias, value_bias, output_bias, inner_bias, outer_bias = full_vectors[:5]
        attn_gain, attn_shift, feed_gain, feed_shift = full_vectors[5:]

        tokens_all, query_mat, key_mat, value_mat = assemble(pack_pieces, (rows, shard, shard, shard))
        queries = (mat_dot(hidden, query_mat) + query_bias).astype(LOW)
        group_keys = mat_dot(tokens_all, key_mat).astype(LOW)
        group_values = (mat_dot(tokens_all, value_mat) + value_bias).astype(LOW)
        position = jnp.stack([prefix[rep], (group * rows).astype(jnp.int32)])
        new_logits, probs, context = attend(position, queries, group_keys, group_values, prev_logits)
        (output_mat,) = assemble(output_pieces, (shard,))
        (inner_mat,) = assemble(inner_pieces, (shard,))
        (outer_mat,) = assemble(outer_pieces, (feed_shard,))

        attn_out = mat_dot(context, output_mat) + output_bias
        first_out, first_norm, first_scale = layer_norm(hidden.astype(F32) + attn_out, attn_gain, attn_shift)
        first_low = first_out.astype(LOW)
        inner_act = mat_dot(first_low, inner_mat) + inner_bias
        gelu_out, gelu_pull = jax.vjp(jax.nn.gelu, inner_act)
        middle, slope = lax.optimization_barrier((gelu_out.astype(LOW), gelu_pull(jnp.ones_like(inner_act))[0]))
        feed_out = mat_dot(middle, outer_mat) + outer_bias
        output, second_norm, second_scale = layer_norm(first_low.astype(F32) + feed_out, feed_gain, feed_shift)
        grad_second, grad_gfeed, grad_sfeed = norm_back(
            out_grad.astype(F32), second_norm, second_scale, feed_gain
        )
        grad_feed = lax.optimization_barrier(grad_second.astype(LOW))
        grad_bouter = jnp.sum(grad_feed.astype(F32), axis=0)

        def reduce_group(value):
            split = value.astype(LOW).reshape((2, 2, -1) + value.shape[1:])
            sent, kept = pick(split, 1 - core, 1), pick(split, core, 1)
            parts = [kept, swap(sent, "grp", 1)]
            return shrink(parts, "grp", 2, far_bit)

        grad_wouter = left_dot(middle, grad_feed)
        outer_pair = reduce_rep(reduce_group(grad_wouter), bits)
        grad_inner = (right_dot(grad_feed, outer_mat) * slope).astype(LOW)
        grad_inner = lax.optimization_barrier(grad_inner)
        grad_binner = jnp.sum(grad_inner.astype(F32), axis=0)
        grad_winner = left_dot(first_low, grad_inner)
        inner_pair = reduce_rep(reduce_group(grad_winner), bits)
        grad_first = grad_second + right_dot(grad_inner, inner_mat)
        grad_resid, grad_gattn, grad_sattn = norm_back(grad_first, first_norm, first_scale, attn_gain)
        grad_attn = lax.optimization_barrier(grad_resid.astype(LOW))
        grad_boutput = jnp.sum(grad_attn.astype(F32), axis=0)
        grad_context = right_dot(grad_attn, output_mat).astype(LOW)
        grad_scores, grad_queries, grad_keys, grad_values = attend_back(
            queries, group_keys, group_values, probs, logit_grad, grad_context
        )
        grad_bquery = jnp.sum(grad_queries.astype(F32), axis=0)
        grad_bvalue = jnp.sum(grad_values.astype(F32), axis=0)
        grad_woutput = left_dot(context, grad_attn)
        grad_wquery = left_dot(hidden, grad_queries)
        grad_wkey = left_dot(tokens_all, grad_keys)
        grad_wvalue = left_dot(tokens_all, grad_values)
        grad_own = grad_resid + right_dot(grad_queries, query_mat)
        grad_rows = (right_dot(grad_keys, key_mat) + right_dot(grad_values, value_mat)).astype(LOW)

        vec_grads = (
            grad_bquery,
            grad_bvalue,
            grad_boutput,
            grad_binner,
            grad_bouter,
            grad_gattn,
            grad_sattn,
            grad_gfeed,
            grad_sfeed,
        )
        vec_sum = jnp.concatenate([item.reshape(4, -1) for item in vec_grads], axis=1)
        vec_sum = vec_sum + swap(vec_sum, "grp", 1)
        vec_sum = pick(vec_sum.reshape(2, 2, vec_count), core, 1)
        vec_sum = pick(vec_sum, far_bit) + swap(pick(vec_sum, 1 - far_bit), "grp", 2)
        for step, _ in bits:
            vec_sum = vec_sum + swap(vec_sum, "rep", step)

        sent, kept = split_by_core(
            [
                item.astype(LOW).reshape(2, 2, -1, width)
                for item in (grad_wquery, grad_wkey, grad_wvalue, grad_woutput, grad_rows)
            ]
        )
        attn_parts = [kept, swap(sent, "grp", 1)]
        attn_parts = shrink(attn_parts, "grp", 2, far_bit)
        grad_input = grad_own + summed([part[4 * shard :] for part in attn_parts])
        mine, other = reduce_rep([part[: 4 * shard] for part in attn_parts], bits)
        low_bit = bits[0][1]
        attn_grads = []
        for k in range(4):
            cut = slice((k % 2) * shard, (k % 2 + 1) * shard)
            attn_grads.append(jnp.where(low_bit == k // 2, mine[cut], other[cut]).astype(F32))
        vec_outs = []
        offset = 0
        for size in vec_sizes:
            vec_outs.append(vec_sum[offset : offset + size])
            offset += size
        return (
            output.astype(LOW),
            new_logits,
            grad_input.astype(LOW),
            grad_scores,
            *attn_grads,
            finish(inner_pair, bits),
            finish(outer_pair, bits),
            *vec_outs,
        )

    return inner_body


def solution(mesh):
    rows = P(("rep", "grp"), None)
    logits = P(None, ("rep", "grp"), None)
    matrix = P("grp", None)
    vector = P("grp")
    return jax.shard_map(
        make_body(mesh.shape["rep"], mesh.shape["grp"]),
        mesh=mesh,
        in_specs=(rows, logits, P(), *(matrix,) * 6, *(vector,) * 9, rows, logits),
        out_specs=(rows, logits, rows, logits, *(matrix,) * 6, *(vector,) * 9),
        check_vma=False,
    )
```

```python
import jax
import jax.numpy as jnp
from jax import lax
from jax.experimental import pallas as pl
from jax.experimental.pallas import tpu as pltpu
from jax.sharding import PartitionSpec as P


HEADS = 12
epsilon = 1e-06
LOW = jnp.bfloat16
F32 = jnp.float32
ANY = pl.BlockSpec(memory_space=pl.ANY)
INSIDE = pl.BlockSpec(memory_space=pltpu.VMEM)


def mat_dot(left, right):
    return jnp.dot(left, right, preferred_element_type=F32)


def left_dot(left, right):
    return lax.dot_general(left, right, (((0,), (0,)), ((), ())), preferred_element_type=F32)


def right_dot(left, right):
    return lax.dot_general(left, right, (((1,), (1,)), ((), ())), preferred_element_type=F32)


def layer_norm(values, gain, shift):
    center = values - jnp.mean(values, axis=-1, keepdims=True)
    spread = jnp.mean(center * center, axis=-1, keepdims=True)
    scale = lax.rsqrt(spread + epsilon)
    normed = center * scale
    return (normed * gain + shift, normed, scale)


def norm_back(grad_out, normed, scale, gain):
    grad_norm = grad_out * gain
    grad_in = scale * (
        grad_norm
        - jnp.mean(grad_norm, axis=-1, keepdims=True)
        - normed * jnp.mean(grad_norm * normed, axis=-1, keepdims=True)
    )
    return (grad_in, jnp.sum(grad_out * normed, axis=0), jnp.sum(grad_out, axis=0))


def run_copies(copies, sems):
    started = [pltpu.make_async_copy(a, b, sems.at[i]) for i, (a, b) in enumerate(copies)]
    for copy in started:
        copy.start()
    for copy in started:
        copy.wait()


def pack_rows(parts):
    counts = [part.shape[0] for part in parts]
    width = parts[0].shape[1]

    def kernel(*refs):
        ins, out, sems = refs[: len(parts)], refs[-2], refs[-1]
        copies = []
        start = 0
        for ref, count in zip(ins, counts):
            copies.append((ref, out.at[pl.ds(start, count)]))
            start += count
        run_copies(copies, sems)

    return pl.pallas_call(
        kernel,
        out_shape=jax.ShapeDtypeStruct((sum(counts), width), parts[0].dtype),
        in_specs=[ANY] * len(parts),
        out_specs=INSIDE,
        scratch_shapes=[pltpu.SemaphoreType.DMA((len(parts),))],
    )(*parts)


def assemble(pieces, counts):
    arrays = [piece[0] for piece in pieces]
    width = arrays[0].shape[1]

    def kernel(*refs):
        ins, outs, sems = refs[: len(arrays)], refs[len(arrays) : -1], refs[-1]
        me = lax.axis_index("grp")
        low = lax.axis_index("rep") & 1
        copies = []
        for ref, (_, step, half) in zip(ins, pieces):
            start = 0
            for out, count in zip(outs, counts):
                rows = count if half is None else count // 2
                at = (me ^ step) * count
                if half is not None:
                    at = at + (low ^ half) * rows
                copies.append((ref.at[pl.ds(start, rows)], out.at[pl.ds(pl.multiple_of(at, 32), rows)]))
                start += rows
        run_copies(copies, sems)

    return pl.pallas_call(
        kernel,
        out_shape=[jax.ShapeDtypeStruct((4 * count, width), arrays[0].dtype) for count in counts],
        in_specs=[ANY] * len(arrays),
        out_specs=[INSIDE] * len(counts),
        scratch_shapes=[pltpu.SemaphoreType.DMA((len(arrays) * len(counts),))],
    )(*arrays)


def send_rows(parts):
    counts = [part.shape[2] for part in parts]
    width = parts[0].shape[3]

    def kernel(*refs):
        ins, out, sems = refs[: len(parts)], refs[-2], refs[-1]
        other = 1 - (lax.axis_index("grp") & 1)
        copies = []
        start = 0
        for ref, count in zip(ins, counts):
            for far in range(2):
                copies.append((ref.at[far, other], out.at[far, pl.ds(start, count)]))
            start += count
        run_copies(copies, sems)

    return pl.pallas_call(
        kernel,
        out_shape=jax.ShapeDtypeStruct((2, sum(counts), width), parts[0].dtype),
        in_specs=[ANY] * len(parts),
        out_specs=INSIDE,
        scratch_shapes=[pltpu.SemaphoreType.DMA((2 * len(parts),))],
    )(*parts)


def halve_first(parts, got, cuts):
    counts = [part.shape[2] for part in parts]
    total, width = got.shape[1:]

    def kernel(*refs):
        ins, outs = refs[: len(parts) + 1], refs[len(parts) + 1 : -3]
        own, come, sems = refs[-3:]
        me = lax.axis_index("grp")
        core, far = me & 1, me >> 1
        copies = [(ins[-1], come)]
        start = 0
        for ref, count in zip(ins, counts):
            for side in range(2):
                copies.append((ref.at[side, core], own.at[side, pl.ds(start, count)]))
            start += count
        run_copies(copies, sems)
        start = 0
        for k, count in enumerate(cuts):
            rows = pl.ds(start, count)
            for out, side in ((outs[2 * k], 1 - far), (outs[2 * k + 1], far)):
                out[...] = (own[side, rows].astype(F32) + come[side, rows].astype(F32)).astype(LOW)
            start += count

    return pl.pallas_call(
        kernel,
        out_shape=[jax.ShapeDtypeStruct((count, width), LOW) for count in cuts for _ in range(2)],
        in_specs=[ANY] * (len(parts) + 1),
        out_specs=[INSIDE] * (2 * len(cuts)),
        scratch_shapes=[pltpu.VMEM((2, total, width), LOW)] * 2 + [pltpu.SemaphoreType.DMA((2 * len(parts) + 1,))],
    )(*parts, got)


def halve(kept, got, step):
    kept, got = [part.reshape((2, part.shape[0] // 2) + part.shape[1:]) for part in (kept, got)]

    def kernel(kept_ref, got_ref, sent, rest):
        side = (lax.axis_index("rep") // step) & 1
        sent[...] = (kept_ref[1 - side].astype(F32) + got_ref[1 - side].astype(F32)).astype(LOW)
        rest[...] = (kept_ref[side].astype(F32) + got_ref[side].astype(F32)).astype(LOW)

    shape = jax.ShapeDtypeStruct(kept.shape[1:], LOW)
    return pl.pallas_call(
        kernel, out_shape=[shape, shape], in_specs=[INSIDE, INSIDE], out_specs=[INSIDE, INSIDE]
    )(kept, got)


def add_low(kept, got):
    def kernel(kept_ref, got_ref, out):
        out[...] = (kept_ref[...].astype(F32) + got_ref[...].astype(F32)).astype(LOW)

    return pl.pallas_call(
        kernel, out_shape=jax.ShapeDtypeStruct(kept.shape, LOW), in_specs=[INSIDE, INSIDE], out_specs=INSIDE
    )(kept, got)


def join(mine, other, step, dtype):
    def kernel(mine_ref, other_ref, out):
        side = (lax.axis_index("rep") // step) & 1
        out[side] = mine_ref[...].astype(dtype)
        out[1 - side] = other_ref[...].astype(dtype)

    both = pl.pallas_call(
        kernel,
        out_shape=jax.ShapeDtypeStruct((2,) + mine.shape, dtype),
        in_specs=[INSIDE, INSIDE],
        out_specs=INSIDE,
    )(mine, other)
    return both.reshape((2 * mine.shape[0],) + mine.shape[1:])


def spread(mine, other, counts):
    half, width = mine.shape

    def kernel(mine_ref, other_ref, *outs):
        side = lax.axis_index("rep") & 1
        for low in range(2):

            @pl.when(side == low)
            def _():
                start = 0
                for out, count in zip(outs, counts):
                    for k in range(2):
                        first, last = max(start, k * half), min(start + count, (k + 1) * half)
                        if first < last:
                            ref = mine_ref if k == low else other_ref
                            out[pl.ds(first - start, last - first)] = ref[pl.ds(first - k * half, last - first)].astype(F32)
                    start += count

    return pl.pallas_call(
        kernel,
        out_shape=[jax.ShapeDtypeStruct((count, width), F32) for count in counts],
        in_specs=[INSIDE, INSIDE],
        out_specs=[INSIDE] * len(counts),
    )(mine, other)


def nt_dot(left, right):
    return lax.dot_general(left, right, (((1,), (1,)), ((), ())), preferred_element_type=F32)


def nn_dot(left, right):
    return lax.dot_general(left, right, (((1,), (0,)), ((), ())), preferred_element_type=F32)


def attend(place, queries, keys, values, prev_logits):
    rows, width = queries.shape
    length = keys.shape[0]
    head_dim = width // HEADS
    each = 128 // head_dim
    cols = each * head_dim

    def kernel(place_ref, q_ref, k_ref, v_ref, prev_ref, new_ref, prob_ref, ctx_ref):
        lane = lax.broadcasted_iota(jnp.int32, (rows, cols), 1)
        key_pos = lax.broadcasted_iota(jnp.int32, (rows, length), 1)
        query_pos = place_ref[1] + lax.broadcasted_iota(jnp.int32, (rows, length), 0)
        allowed = (key_pos < place_ref[0]) | (key_pos <= query_pos)
        q = q_ref[...].astype(F32) * 0.125
        k = k_ref[...]
        v = v_ref[...]
        context = jnp.zeros((rows, cols), F32)
        for h in range(each):
            mine = (lane >= h * head_dim) & (lane < (h + 1) * head_dim)
            scores = nt_dot(jnp.where(mine, q, 0.0).astype(LOW), k) + prev_ref[h].astype(F32)
            new_ref[h] = scores.astype(LOW)
            scores = jnp.where(allowed, scores, -1e30)
            terms = jnp.exp(scores - jnp.max(scores, axis=-1, keepdims=True))
            probs = (terms * (1.0 / jnp.sum(terms, axis=-1, keepdims=True))).astype(LOW)
            prob_ref[h] = probs
            context = jnp.where(mine, nn_dot(probs, v), context)
        ctx_ref[...] = context.astype(LOW)

    tall = pl.BlockSpec((length, cols), lambda i: (0, i))
    wide = pl.BlockSpec((rows, cols), lambda i: (0, i))
    square = pl.BlockSpec((each, rows, length), lambda i: (i, 0, 0))
    squares = jax.ShapeDtypeStruct((HEADS, rows, length), LOW)
    return pl.pallas_call(
        kernel,
        grid=(HEADS // each,),
        out_shape=[squares, squares, jax.ShapeDtypeStruct((rows, width), LOW)],
        in_specs=[pl.BlockSpec(memory_space=pltpu.SMEM), wide, tall, tall, square],
        out_specs=[square, square, wide],
    )(place, queries, keys, values, prev_logits)


def attend_back(queries, keys, values, probs, logit_grad, grad_context):
    rows, width = queries.shape
    length = keys.shape[0]
    head_dim = width // HEADS
    each = 128 // head_dim
    cols = each * head_dim

    def kernel(q_ref, k_ref, v_ref, prob_ref, lg_ref, dc_ref, ds_ref, dq_ref, dk_ref, dv_ref):
        lane = lax.broadcasted_iota(jnp.int32, (rows, cols), 1)
        dc = dc_ref[...].astype(F32)
        dc_turned = dc.T.astype(LOW)
        q_turned = (q_ref[...].astype(F32) * 0.125).T.astype(LOW)
        k = k_ref[...]
        v = v_ref[...]
        dq = jnp.zeros((rows, cols), F32)
        dk, dv = [], []
        for h in range(each):
            own = slice(h * head_dim, (h + 1) * head_dim)
            mine = (lane >= h * head_dim) & (lane < (h + 1) * head_dim)
            prob_low = prob_ref[h]
            prob = prob_low.astype(F32)
            dp = nt_dot(jnp.where(mine, dc, 0.0).astype(LOW), v)
            ds = prob * (dp - jnp.sum(dp * prob, axis=-1, keepdims=True)) + lg_ref[h].astype(F32)
            ds = ds.astype(LOW)
            ds_ref[h] = ds
            dq = jnp.where(mine, nn_dot(ds, k), dq)
            dv.append(nn_dot(dc_turned[own], prob_low))
            dk.append(nn_dot(q_turned[own], ds))
        dq_ref[...] = (dq * 0.125).astype(LOW)
        dk_ref[...] = jnp.concatenate(dk, axis=0).T.astype(LOW)
        dv_ref[...] = jnp.concatenate(dv, axis=0).T.astype(LOW)

    tall = pl.BlockSpec((length, cols), lambda i: (0, i))
    wide = pl.BlockSpec((rows, cols), lambda i: (0, i))
    square = pl.BlockSpec((each, rows, length), lambda i: (i, 0, 0))
    talls = jax.ShapeDtypeStruct((length, width), LOW)
    return pl.pallas_call(
        kernel,
        grid=(HEADS // each,),
        out_shape=[jax.ShapeDtypeStruct((HEADS, rows, length), LOW), jax.ShapeDtypeStruct((rows, width), LOW), talls, talls],
        in_specs=[wide, tall, tall, square, square, wide],
        out_specs=[square, wide, tall, tall],
    )(queries, keys, values, probs, logit_grad, grad_context)


def make_body(rep_size, grp_size):
    def swap(value, axis, bit):
        size = rep_size if axis == "rep" else grp_size
        return lax.ppermute(value, axis, [(i, i ^ bit) for i in range(size)])

    def pick(value, index, axis=0):
        return lax.dynamic_index_in_dim(value, index, axis, keepdims=False)

    def gather_group(shard):
        far = swap(shard, "grp", 2)
        near = swap(shard, "grp", 1)
        diag = swap(far, "grp", 1)
        return (shard, 0, None), (near, 1, None), (far, 2, None), (diag, 3, None)

    def gather_halves(shard, low):
        half = pick(in_two(shard), low)
        near = swap(shard, "grp", 1)
        far = swap(half, "grp", 2)
        side = swap(far, "rep", 1)
        diag = swap(far, "grp", 1)
        last = swap(side, "grp", 1)
        return (shard, 0, None), (near, 1, None), (far, 2, 0), (side, 2, 1), (diag, 3, 0), (last, 3, 1)

    def rep_bits(rep):
        count = rep_size.bit_length() - 1
        return [(1 << k, (rep >> k) & 1) for k in range(count)]

    def in_two(part):
        return part.reshape((2, part.shape[0] // 2) + part.shape[1:])

    def reduce_group(values, cuts=None):
        split = [value.reshape((2, 2, value.shape[0] // 4) + value.shape[1:]) for value in values]
        got = swap(send_rows(split), "grp", 1)
        halves = halve_first(split, got, cuts or (split[0].shape[2],))
        return halves[1], swap(halves[0], "grp", 2), *halves[2:]

    def reduce_rep(kept, got, bits):
        for step, _ in bits[:-1]:
            sent, kept = halve(kept, got, step)
            got = swap(sent, "rep", step)
        value = add_low(kept, got)
        step = bits[-1][0]
        value = add_low(value, swap(value, "rep", step))
        for step, _ in reversed(bits[1:-1]):
            value = join(value, swap(value, "rep", step), step, LOW)
        return value, swap(value, "rep", 1)

    def inner_body(
        hidden,
        prev_logits,
        prefix,
        w_query,
        w_key,
        w_value,
        w_output,
        w_inner,
        w_outer,
        b_query,
        b_value,
        b_output,
        b_inner,
        b_outer,
        gain_attn,
        shift_attn,
        gain_feed,
        shift_feed,
        out_grad,
        logit_grad,
    ):
        rows, width = hidden.shape
        shard = w_query.shape[0]
        feed_shard = w_outer.shape[0]
        rep = lax.axis_index("rep")
        group = lax.axis_index("grp")
        bits = rep_bits(rep)
        pack = pack_rows((hidden, w_query, w_key, w_value))
        pack_pieces = gather_group(pack)
        vectors = (b_query, b_value, b_output, b_inner, b_outer, gain_attn, shift_attn, gain_feed, shift_feed)
        vec_sizes = [item.shape[0] for item in vectors]
        vec_count = sum(vec_sizes)
        vec = jnp.concatenate(vectors)
        vec_pieces = gather_group(vec)
        output_pieces = gather_group(w_output)
        inner_pieces = gather_halves(w_inner, rep & 1)
        outer_pieces = gather_halves(w_outer, rep & 1)

        vec_all = jnp.zeros((4, vec_count), F32)
        for piece, step, _ in vec_pieces:
            vec_all = lax.dynamic_update_index_in_dim(vec_all, piece.astype(F32), group ^ step, 0)
        full_vectors = []
        offset = 0
        for size in vec_sizes:
            full_vectors.append(vec_all[:, offset : offset + size].reshape(4 * size))
            offset += size
        query_bias, value_bias, output_bias, inner_bias, outer_bias = full_vectors[:5]
        attn_gain, attn_shift, feed_gain, feed_shift = full_vectors[5:]

        tokens_all, query_mat, key_mat, value_mat = assemble(pack_pieces, (rows, shard, shard, shard))
        queries = (mat_dot(hidden, query_mat) + query_bias).astype(LOW)
        group_keys = mat_dot(tokens_all, key_mat).astype(LOW)
        group_values = (mat_dot(tokens_all, value_mat) + value_bias).astype(LOW)
        position = jnp.stack([prefix[rep], (group * rows).astype(jnp.int32)])
        new_logits, probs, context = attend(position, queries, group_keys, group_values, prev_logits)
        (output_mat,) = assemble(output_pieces, (shard,))
        (inner_mat,) = assemble(inner_pieces, (shard,))
        (outer_mat,) = assemble(outer_pieces, (feed_shard,))

        attn_out = mat_dot(context, output_mat) + output_bias
        first_out, first_norm, first_scale = layer_norm(hidden.astype(F32) + attn_out, attn_gain, attn_shift)
        first_low = first_out.astype(LOW)
        inner_act = mat_dot(first_low, inner_mat) + inner_bias
        gelu_out, gelu_pull = jax.vjp(jax.nn.gelu, inner_act)
        middle, slope = gelu_out.astype(LOW), gelu_pull(jnp.ones_like(inner_act))[0]
        middle, slope = lax.optimization_barrier((middle, slope))
        feed_out = mat_dot(middle, outer_mat) + outer_bias
        output, second_norm, second_scale = layer_norm(first_low.astype(F32) + feed_out, feed_gain, feed_shift)
        grad_second, grad_gfeed, grad_sfeed = norm_back(
            out_grad.astype(F32), second_norm, second_scale, feed_gain
        )
        grad_feed = lax.optimization_barrier(grad_second.astype(LOW))
        grad_bouter = jnp.sum(grad_feed.astype(F32), axis=0)
        grad_wouter = left_dot(middle, grad_feed).astype(LOW)
        outer_pair = reduce_rep(*reduce_group([grad_wouter]), bits)
        grad_inner = (right_dot(grad_feed, outer_mat) * slope).astype(LOW)
        grad_inner = lax.optimization_barrier(grad_inner)
        grad_binner = jnp.sum(grad_inner.astype(F32), axis=0)
        grad_winner = left_dot(first_low, grad_inner).astype(LOW)
        inner_pair = reduce_rep(*reduce_group([grad_winner]), bits)
        grad_first = grad_second + right_dot(grad_inner, inner_mat)
        grad_resid, grad_gattn, grad_sattn = norm_back(grad_first, first_norm, first_scale, attn_gain)
        grad_attn = lax.optimization_barrier(grad_resid.astype(LOW))
        grad_boutput = jnp.sum(grad_attn.astype(F32), axis=0)
        grad_context = right_dot(grad_attn, output_mat).astype(LOW)
        grad_scores, grad_queries, grad_keys, grad_values = attend_back(
            queries, group_keys, group_values, probs, logit_grad, grad_context
        )
        grad_bquery = jnp.sum(grad_queries.astype(F32), axis=0)
        grad_bvalue = jnp.sum(grad_values.astype(F32), axis=0)
        grad_woutput = left_dot(context, grad_attn)
        grad_wquery = left_dot(hidden, grad_queries)
        grad_wkey = left_dot(tokens_all, grad_keys)
        grad_wvalue = left_dot(tokens_all, grad_values)
        grad_rows = (right_dot(grad_keys, key_mat) + right_dot(grad_values, value_mat)).astype(LOW)

        grad_own = grad_resid + right_dot(grad_queries, query_mat)

        vec_grads = (
            grad_bquery,
            grad_bvalue,
            grad_boutput,
            grad_binner,
            grad_bouter,
            grad_gattn,
            grad_sattn,
            grad_gfeed,
            grad_sfeed,
        )
        vec_rows = vec_count // width
        vec_value = jnp.concatenate([item.reshape(4, -1) for item in vec_grads], axis=1).reshape(4, vec_rows, width)
        vec_value = jnp.pad(vec_value, ((0, 0), (0, 64 - vec_rows), (0, 0))).reshape(256, width)

        attn_values = [item.astype(LOW) for item in (grad_wquery, grad_wkey, grad_wvalue, grad_woutput, vec_value, grad_rows)]
        counts = (shard,) * 4 + (64,)
        kept, got, rows_sent, rows_kept = reduce_group(attn_values, (sum(counts), rows))
        rows_got = swap(rows_sent, "grp", 2)
        grad_input = grad_own + rows_kept.astype(F32) + rows_got.astype(F32)
        *attn_grads, vec_sum = spread(*reduce_rep(kept, got, bits), counts)
        vec_sum = vec_sum[:vec_rows].reshape(vec_count)
        vec_outs = []
        offset = 0
        for size in vec_sizes:
            vec_outs.append(vec_sum[offset : offset + size])
            offset += size
        return (
            output.astype(LOW),
            new_logits,
            grad_input.astype(LOW),
            grad_scores,
            *attn_grads,
            join(*inner_pair, 1, F32),
            join(*outer_pair, 1, F32),
            *vec_outs,
        )

    return inner_body


def solution(mesh):
    rows = P(("rep", "grp"), None)
    logits = P(None, ("rep", "grp"), None)
    matrix = P("grp", None)
    vector = P("grp")
    return jax.shard_map(
        make_body(mesh.shape["rep"], mesh.shape["grp"]),
        mesh=mesh,
        in_specs=(rows, logits, P(), *(matrix,) * 6, *(vector,) * 9, rows, logits),
        out_specs=(rows, logits, rows, logits, *(matrix,) * 6, *(vector,) * 9),
        check_vma=False,
    )
```

```python
import jax
import jax.numpy as jnp
from jax import lax
from jax.experimental import pallas as pl
from jax.experimental.pallas import tpu as pltpu
from jax.sharding import PartitionSpec as P


HEADS = 12
epsilon = 1e-06
LOW = jnp.bfloat16
F32 = jnp.float32
ANY = pl.BlockSpec(memory_space=pl.ANY)
INSIDE = pl.BlockSpec(memory_space=pltpu.VMEM)


def mat_dot(left, right):
    return jnp.dot(left, right, preferred_element_type=F32)


def left_dot(left, right):
    return lax.dot_general(left, right, (((0,), (0,)), ((), ())), preferred_element_type=F32)


def right_dot(left, right):
    return lax.dot_general(left, right, (((1,), (1,)), ((), ())), preferred_element_type=F32)


def layer_norm(values, gain, shift):
    center = values - jnp.mean(values, axis=-1, keepdims=True)
    spread = jnp.mean(center * center, axis=-1, keepdims=True)
    scale = lax.rsqrt(spread + epsilon)
    normed = center * scale
    return (normed * gain + shift, normed, scale)


def norm_back(grad_out, normed, scale, gain):
    grad_norm = grad_out * gain
    grad_in = scale * (
        grad_norm
        - jnp.mean(grad_norm, axis=-1, keepdims=True)
        - normed * jnp.mean(grad_norm * normed, axis=-1, keepdims=True)
    )
    return (grad_in, jnp.sum(grad_out * normed, axis=0, keepdims=True), jnp.sum(grad_out, axis=0, keepdims=True))


def run_copies(copies, sems):
    started = [pltpu.make_async_copy(a, b, sems.at[i]) for i, (a, b) in enumerate(copies)]
    for copy in started:
        copy.start()
    for copy in started:
        copy.wait()


def pack_rows(parts):
    counts = [part.shape[0] for part in parts]
    width = parts[0].shape[1]

    def kernel(*refs):
        ins, out, sems = refs[: len(parts)], refs[-2], refs[-1]
        copies = []
        start = 0
        for ref, count in zip(ins, counts):
            copies.append((ref, out.at[pl.ds(start, count)]))
            start += count
        run_copies(copies, sems)

    return pl.pallas_call(
        kernel,
        out_shape=jax.ShapeDtypeStruct((sum(counts), width), parts[0].dtype),
        in_specs=[ANY] * len(parts),
        out_specs=INSIDE,
        scratch_shapes=[pltpu.SemaphoreType.DMA((len(parts),))],
    )(*parts)


def assemble(pieces, counts):
    arrays = [piece[0] for piece in pieces]
    width = arrays[0].shape[1]

    def kernel(*refs):
        ins, outs, sems = refs[: len(arrays)], refs[len(arrays) : -1], refs[-1]
        me = lax.axis_index("grp")
        low = lax.axis_index("rep") & 1
        copies = []
        for ref, (_, step, half) in zip(ins, pieces):
            start = 0
            for out, count in zip(outs, counts):
                rows = count if half is None else count // 2
                at = (me ^ step) * count
                if half is not None:
                    at = at + (low ^ half) * rows
                copies.append((ref.at[pl.ds(start, rows)], out.at[pl.ds(pl.multiple_of(at, 32), rows)]))
                start += rows
        run_copies(copies, sems)

    return pl.pallas_call(
        kernel,
        out_shape=[jax.ShapeDtypeStruct((4 * count, width), arrays[0].dtype) for count in counts],
        in_specs=[ANY] * len(arrays),
        out_specs=[INSIDE] * len(counts),
        scratch_shapes=[pltpu.SemaphoreType.DMA((len(arrays) * len(counts),))],
    )(*arrays)


def block_of(ref, side, core):
    return ref.at[side, core] if len(ref.shape) == 4 else ref


def stack_rows(vectors, rows):
    width = vectors[0].shape[1]

    def kernel(*refs):
        out = refs[-1]
        lines = []
        for ref in refs[:-1]:
            for k in range(ref.shape[1] // width):
                lines.append(ref[:, k * width : (k + 1) * width])
        lines.append(jnp.zeros((rows - len(lines), width), F32))
        out[...] = jnp.concatenate(lines, axis=0).astype(LOW)

    return pl.pallas_call(
        kernel,
        out_shape=jax.ShapeDtypeStruct((rows, width), LOW),
        in_specs=[INSIDE] * len(vectors),
        out_specs=INSIDE,
    )(*vectors)


def send_rows(parts):
    counts = [part.shape[-2] for part in parts]
    width = parts[0].shape[-1]

    def kernel(*refs):
        ins, out, sems = refs[: len(parts)], refs[-2], refs[-1]
        other = 1 - (lax.axis_index("grp") & 1)
        copies = []
        start = 0
        for ref, count in zip(ins, counts):
            for far in range(2):
                copies.append((block_of(ref, far, other), out.at[far, pl.ds(start, count)]))
            start += count
        run_copies(copies, sems)

    return pl.pallas_call(
        kernel,
        out_shape=jax.ShapeDtypeStruct((2, sum(counts), width), parts[0].dtype),
        in_specs=[ANY] * len(parts),
        out_specs=INSIDE,
        scratch_shapes=[pltpu.SemaphoreType.DMA((2 * len(parts),))],
    )(*parts)


def halve_first(parts, got, cuts):
    counts = [part.shape[-2] for part in parts]
    total, width = got.shape[1:]

    def kernel(*refs):
        ins, outs = refs[: len(parts) + 1], refs[len(parts) + 1 : -3]
        own, come, sems = refs[-3:]
        me = lax.axis_index("grp")
        core, far = me & 1, me >> 1
        copies = [(ins[-1], come)]
        start = 0
        for ref, count in zip(ins, counts):
            for side in range(2):
                copies.append((block_of(ref, side, core), own.at[side, pl.ds(start, count)]))
            start += count
        run_copies(copies, sems)
        start = 0
        for k, count in enumerate(cuts):
            rows = pl.ds(start, count)
            for out, side in ((outs[2 * k], 1 - far), (outs[2 * k + 1], far)):
                out[...] = (own[side, rows].astype(F32) + come[side, rows].astype(F32)).astype(LOW)
            start += count

    return pl.pallas_call(
        kernel,
        out_shape=[jax.ShapeDtypeStruct((count, width), LOW) for count in cuts for _ in range(2)],
        in_specs=[ANY] * (len(parts) + 1),
        out_specs=[INSIDE] * (2 * len(cuts)),
        scratch_shapes=[pltpu.VMEM((2, total, width), LOW)] * 2 + [pltpu.SemaphoreType.DMA((2 * len(parts) + 1,))],
    )(*parts, got)


def halve(kept, got, step):
    kept, got = [part.reshape((2, part.shape[0] // 2) + part.shape[1:]) for part in (kept, got)]

    def kernel(kept_ref, got_ref, sent, rest):
        side = (lax.axis_index("rep") // step) & 1
        sent[...] = (kept_ref[1 - side].astype(F32) + got_ref[1 - side].astype(F32)).astype(LOW)
        rest[...] = (kept_ref[side].astype(F32) + got_ref[side].astype(F32)).astype(LOW)

    shape = jax.ShapeDtypeStruct(kept.shape[1:], LOW)
    return pl.pallas_call(
        kernel, out_shape=[shape, shape], in_specs=[INSIDE, INSIDE], out_specs=[INSIDE, INSIDE]
    )(kept, got)


def add_low(kept, got):
    def kernel(kept_ref, got_ref, out):
        out[...] = (kept_ref[...].astype(F32) + got_ref[...].astype(F32)).astype(LOW)

    return pl.pallas_call(
        kernel, out_shape=jax.ShapeDtypeStruct(kept.shape, LOW), in_specs=[INSIDE, INSIDE], out_specs=INSIDE
    )(kept, got)


def join(mine, other, step, dtype):
    def kernel(mine_ref, other_ref, out):
        side = (lax.axis_index("rep") // step) & 1
        out[side] = mine_ref[...].astype(dtype)
        out[1 - side] = other_ref[...].astype(dtype)

    both = pl.pallas_call(
        kernel,
        out_shape=jax.ShapeDtypeStruct((2,) + mine.shape, dtype),
        in_specs=[INSIDE, INSIDE],
        out_specs=INSIDE,
    )(mine, other)
    return both.reshape((2 * mine.shape[0],) + mine.shape[1:])


def spread(mine, other, counts):
    half, width = mine.shape

    def kernel(mine_ref, other_ref, *outs):
        side = lax.axis_index("rep") & 1
        for low in range(2):

            @pl.when(side == low)
            def _():
                start = 0
                for out, count in zip(outs, counts):
                    for k in range(2):
                        first, last = max(start, k * half), min(start + count, (k + 1) * half)
                        if first < last:
                            ref = mine_ref if k == low else other_ref
                            out[pl.ds(first - start, last - first)] = ref[pl.ds(first - k * half, last - first)].astype(F32)
                    start += count

    return pl.pallas_call(
        kernel,
        out_shape=[jax.ShapeDtypeStruct((count, width), F32) for count in counts],
        in_specs=[INSIDE, INSIDE],
        out_specs=[INSIDE] * len(counts),
    )(mine, other)


def nt_dot(left, right):
    return lax.dot_general(left, right, (((1,), (1,)), ((), ())), preferred_element_type=F32)


def nn_dot(left, right):
    return lax.dot_general(left, right, (((1,), (0,)), ((), ())), preferred_element_type=F32)


def attend(place, queries, keys, values, prev_logits):
    rows, width = queries.shape
    length = keys.shape[0]
    head_dim = width // HEADS
    each = 128 // head_dim
    cols = each * head_dim

    def kernel(place_ref, q_ref, k_ref, v_ref, prev_ref, new_ref, prob_ref, ctx_ref):
        lane = lax.broadcasted_iota(jnp.int32, (rows, cols), 1)
        key_pos = lax.broadcasted_iota(jnp.int32, (rows, length), 1)
        query_pos = place_ref[1] + lax.broadcasted_iota(jnp.int32, (rows, length), 0)
        allowed = (key_pos < place_ref[0]) | (key_pos <= query_pos)
        q = q_ref[...].astype(F32) * 0.125
        k = k_ref[...]
        v = v_ref[...]
        context = jnp.zeros((rows, cols), F32)
        for h in range(each):
            mine = (lane >= h * head_dim) & (lane < (h + 1) * head_dim)
            scores = nt_dot(jnp.where(mine, q, 0.0).astype(LOW), k) + prev_ref[h].astype(F32)
            new_ref[h] = scores.astype(LOW)
            scores = jnp.where(allowed, scores, -1e30)
            terms = jnp.exp(scores - jnp.max(scores, axis=-1, keepdims=True))
            probs = (terms * (1.0 / jnp.sum(terms, axis=-1, keepdims=True))).astype(LOW)
            prob_ref[h] = probs
            context = jnp.where(mine, nn_dot(probs, v), context)
        ctx_ref[...] = context.astype(LOW)

    tall = pl.BlockSpec((length, cols), lambda i: (0, i))
    wide = pl.BlockSpec((rows, cols), lambda i: (0, i))
    square = pl.BlockSpec((each, rows, length), lambda i: (i, 0, 0))
    squares = jax.ShapeDtypeStruct((HEADS, rows, length), LOW)
    return pl.pallas_call(
        kernel,
        grid=(HEADS // each,),
        out_shape=[squares, squares, jax.ShapeDtypeStruct((rows, width), LOW)],
        in_specs=[pl.BlockSpec(memory_space=pltpu.SMEM), wide, tall, tall, square],
        out_specs=[square, square, wide],
    )(place, queries, keys, values, prev_logits)


def attend_back(queries, keys, values, probs, logit_grad, grad_context):
    rows, width = queries.shape
    length = keys.shape[0]
    head_dim = width // HEADS
    each = 128 // head_dim
    cols = each * head_dim

    def kernel(q_ref, k_ref, v_ref, prob_ref, lg_ref, dc_ref, ds_ref, dq_ref, dk_ref, dv_ref):
        lane = lax.broadcasted_iota(jnp.int32, (rows, cols), 1)
        dc = dc_ref[...].astype(F32)
        dc_turned = dc.T.astype(LOW)
        q_turned = (q_ref[...].astype(F32) * 0.125).T.astype(LOW)
        k = k_ref[...]
        v = v_ref[...]
        dq = jnp.zeros((rows, cols), F32)
        dk, dv = [], []
        for h in range(each):
            own = slice(h * head_dim, (h + 1) * head_dim)
            mine = (lane >= h * head_dim) & (lane < (h + 1) * head_dim)
            prob_low = prob_ref[h]
            prob = prob_low.astype(F32)
            dp = nt_dot(jnp.where(mine, dc, 0.0).astype(LOW), v)
            ds = prob * (dp - jnp.sum(dp * prob, axis=-1, keepdims=True)) + lg_ref[h].astype(F32)
            ds = ds.astype(LOW)
            ds_ref[h] = ds
            dq = jnp.where(mine, nn_dot(ds, k), dq)
            dv.append(nn_dot(dc_turned[own], prob_low))
            dk.append(nn_dot(q_turned[own], ds))
        dq_ref[...] = (dq * 0.125).astype(LOW)
        dk_ref[...] = jnp.concatenate(dk, axis=0).T.astype(LOW)
        dv_ref[...] = jnp.concatenate(dv, axis=0).T.astype(LOW)

    tall = pl.BlockSpec((length, cols), lambda i: (0, i))
    wide = pl.BlockSpec((rows, cols), lambda i: (0, i))
    square = pl.BlockSpec((each, rows, length), lambda i: (i, 0, 0))
    talls = jax.ShapeDtypeStruct((length, width), LOW)
    return pl.pallas_call(
        kernel,
        grid=(HEADS // each,),
        out_shape=[jax.ShapeDtypeStruct((HEADS, rows, length), LOW), jax.ShapeDtypeStruct((rows, width), LOW), talls, talls],
        in_specs=[wide, tall, tall, square, square, wide],
        out_specs=[square, wide, tall, tall],
    )(queries, keys, values, probs, logit_grad, grad_context)


def make_body(rep_size, grp_size):
    def swap(value, axis, bit):
        size = rep_size if axis == "rep" else grp_size
        return lax.ppermute(value, axis, [(i, i ^ bit) for i in range(size)])

    def pick(value, index, axis=0):
        return lax.dynamic_index_in_dim(value, index, axis, keepdims=False)

    def gather_group(shard):
        far = swap(shard, "grp", 2)
        near = swap(shard, "grp", 1)
        diag = swap(far, "grp", 1)
        return (shard, 0, None), (near, 1, None), (far, 2, None), (diag, 3, None)

    def gather_halves(shard, low):
        half = pick(in_two(shard), low)
        near = swap(shard, "grp", 1)
        far = swap(half, "grp", 2)
        side = swap(far, "rep", 1)
        diag = swap(far, "grp", 1)
        last = swap(side, "grp", 1)
        return (shard, 0, None), (near, 1, None), (far, 2, 0), (side, 2, 1), (diag, 3, 0), (last, 3, 1)

    def rep_bits(rep):
        count = rep_size.bit_length() - 1
        return [(1 << k, (rep >> k) & 1) for k in range(count)]

    def in_two(part):
        return part.reshape((2, part.shape[0] // 2) + part.shape[1:])

    def reduce_group(values, cuts=None, shared=()):
        split = [value.reshape((2, 2, value.shape[0] // 4) + value.shape[1:]) for value in values] + list(shared)
        got = swap(send_rows(split), "grp", 1)
        halves = halve_first(split, got, cuts or (got.shape[1],))
        return halves[1], swap(halves[0], "grp", 2), *halves[2:]

    def reduce_rep(kept, got, bits):
        for step, _ in bits[:-1]:
            sent, kept = halve(kept, got, step)
            got = swap(sent, "rep", step)
        value = add_low(kept, got)
        step = bits[-1][0]
        value = add_low(value, swap(value, "rep", step))
        for step, _ in reversed(bits[1:-1]):
            value = join(value, swap(value, "rep", step), step, LOW)
        return value, swap(value, "rep", 1)

    def inner_body(
        hidden,
        prev_logits,
        prefix,
        w_query,
        w_key,
        w_value,
        w_output,
        w_inner,
        w_outer,
        b_query,
        b_value,
        b_output,
        b_inner,
        b_outer,
        gain_attn,
        shift_attn,
        gain_feed,
        shift_feed,
        out_grad,
        logit_grad,
    ):
        rows, width = hidden.shape
        shard = w_query.shape[0]
        feed_shard = w_outer.shape[0]
        rep = lax.axis_index("rep")
        group = lax.axis_index("grp")
        bits = rep_bits(rep)
        pack = pack_rows((hidden, w_query, w_key, w_value))
        pack_pieces = gather_group(pack)
        vectors = (b_query, b_value, b_output, b_inner, b_outer, gain_attn, shift_attn, gain_feed, shift_feed)
        vec_sizes = [item.shape[0] for item in vectors]
        vec_count = sum(vec_sizes)
        vec = jnp.concatenate(vectors)
        vec_pieces = gather_group(vec)
        output_pieces = gather_group(w_output)
        inner_pieces = gather_halves(w_inner, rep & 1)
        outer_pieces = gather_halves(w_outer, rep & 1)

        vec_all = jnp.zeros((4, vec_count), F32)
        for piece, step, _ in vec_pieces:
            vec_all = lax.dynamic_update_index_in_dim(vec_all, piece.astype(F32), group ^ step, 0)
        full_vectors = []
        offset = 0
        for size in vec_sizes:
            full_vectors.append(vec_all[:, offset : offset + size].reshape(4 * size))
            offset += size
        query_bias, value_bias, output_bias, inner_bias, outer_bias = full_vectors[:5]
        attn_gain, attn_shift, feed_gain, feed_shift = full_vectors[5:]

        tokens_all, query_mat, key_mat, value_mat = assemble(pack_pieces, (rows, shard, shard, shard))
        queries = (mat_dot(hidden, query_mat) + query_bias).astype(LOW)
        group_keys = mat_dot(tokens_all, key_mat).astype(LOW)
        group_values = (mat_dot(tokens_all, value_mat) + value_bias).astype(LOW)
        position = jnp.stack([prefix[rep], (group * rows).astype(jnp.int32)])
        new_logits, probs, context = attend(position, queries, group_keys, group_values, prev_logits)
        (output_mat,) = assemble(output_pieces, (shard,))
        (inner_mat,) = assemble(inner_pieces, (shard,))
        (outer_mat,) = assemble(outer_pieces, (feed_shard,))

        attn_out = mat_dot(context, output_mat) + output_bias
        first_out, first_norm, first_scale = layer_norm(hidden.astype(F32) + attn_out, attn_gain, attn_shift)
        first_low = first_out.astype(LOW)
        inner_act = mat_dot(first_low, inner_mat) + inner_bias
        gelu_out, gelu_pull = jax.vjp(jax.nn.gelu, inner_act)
        middle, slope = gelu_out.astype(LOW), gelu_pull(jnp.ones_like(inner_act))[0]
        middle, slope = lax.optimization_barrier((middle, slope))
        feed_out = mat_dot(middle, outer_mat) + outer_bias
        output, second_norm, second_scale = layer_norm(first_low.astype(F32) + feed_out, feed_gain, feed_shift)
        grad_second, grad_gfeed, grad_sfeed = norm_back(
            out_grad.astype(F32), second_norm, second_scale, feed_gain
        )
        grad_feed = lax.optimization_barrier(grad_second.astype(LOW))
        grad_bouter = jnp.sum(grad_feed.astype(F32), axis=0, keepdims=True)
        grad_wouter = left_dot(middle, grad_feed).astype(LOW)
        outer_pair = reduce_rep(*reduce_group([grad_wouter]), bits)
        grad_inner = (right_dot(grad_feed, outer_mat) * slope).astype(LOW)
        grad_inner = lax.optimization_barrier(grad_inner)
        grad_binner = jnp.sum(grad_inner.astype(F32), axis=0, keepdims=True)
        grad_winner = left_dot(first_low, grad_inner).astype(LOW)
        inner_pair = reduce_rep(*reduce_group([grad_winner]), bits)
        grad_first = grad_second + right_dot(grad_inner, inner_mat)
        grad_resid, grad_gattn, grad_sattn = norm_back(grad_first, first_norm, first_scale, attn_gain)
        grad_attn = lax.optimization_barrier(grad_resid.astype(LOW))
        grad_boutput = jnp.sum(grad_attn.astype(F32), axis=0, keepdims=True)
        grad_context = right_dot(grad_attn, output_mat).astype(LOW)
        grad_scores, grad_queries, grad_keys, grad_values = attend_back(
            queries, group_keys, group_values, probs, logit_grad, grad_context
        )
        grad_bquery = jnp.sum(grad_queries.astype(F32), axis=0, keepdims=True)
        grad_bvalue = jnp.sum(grad_values.astype(F32), axis=0, keepdims=True)
        grad_woutput = left_dot(context, grad_attn)
        grad_wquery = left_dot(hidden, grad_queries)
        grad_wkey = left_dot(tokens_all, grad_keys)
        grad_wvalue = left_dot(tokens_all, grad_values)
        grad_rows = (right_dot(grad_keys, key_mat) + right_dot(grad_values, value_mat)).astype(LOW)

        grad_own = grad_resid + right_dot(grad_queries, query_mat)

        vec_grads = (
            grad_bquery,
            grad_bvalue,
            grad_boutput,
            grad_binner,
            grad_bouter,
            grad_gattn,
            grad_sattn,
            grad_gfeed,
            grad_sfeed,
        )
        vec_rows = 32
        vec_value = stack_rows(vec_grads, vec_rows)
        attn_values = [item.astype(LOW) for item in (grad_rows, grad_wquery, grad_wkey, grad_wvalue, grad_woutput)]
        counts = (shard,) * 4 + (vec_rows,)
        rows_kept, rows_got, sent, kept = reduce_group(attn_values, (rows, sum(counts)), (vec_value,))
        grad_input = grad_own + rows_kept.astype(F32) + rows_got.astype(F32)
        got = swap(sent, "grp", 2)
        *attn_grads, vec_sum = spread(*reduce_rep(kept, got, bits), counts)
        vec_outs = []
        offset = 0
        for size in vec_sizes:
            lines = 4 * size // width
            whole = vec_sum[offset : offset + lines].reshape(4 * size)
            vec_outs.append(lax.dynamic_slice_in_dim(whole, group * size, size))
            offset += lines
        return (
            output.astype(LOW),
            new_logits,
            grad_input.astype(LOW),
            grad_scores,
            *attn_grads,
            join(*inner_pair, 1, F32),
            join(*outer_pair, 1, F32),
            *vec_outs,
        )

    return inner_body


def solution(mesh):
    rows = P(("rep", "grp"), None)
    logits = P(None, ("rep", "grp"), None)
    matrix = P("grp", None)
    vector = P("grp")
    return jax.shard_map(
        make_body(mesh.shape["rep"], mesh.shape["grp"]),
        mesh=mesh,
        in_specs=(rows, logits, P(), *(matrix,) * 6, *(vector,) * 9, rows, logits),
        out_specs=(rows, logits, rows, logits, *(matrix,) * 6, *(vector,) * 9),
        check_vma=False,
    )
```

```python
import jax
import jax.numpy as jnp
from jax import lax
from jax.experimental import pallas as pl
from jax.experimental.pallas import tpu as pltpu
from jax.sharding import PartitionSpec as P


HEADS = 12
epsilon = 1e-06
LOW = jnp.bfloat16
F32 = jnp.float32
ANY = pl.BlockSpec(memory_space=pl.ANY)
INSIDE = pl.BlockSpec(memory_space=pltpu.VMEM)


def mat_dot(left, right):
    return jnp.dot(left, right, preferred_element_type=F32)


def left_dot(left, right):
    return lax.dot_general(left, right, (((0,), (0,)), ((), ())), preferred_element_type=F32)


def right_dot(left, right):
    return lax.dot_general(left, right, (((1,), (1,)), ((), ())), preferred_element_type=F32)


def layer_norm(values, gain, shift):
    center = values - jnp.mean(values, axis=-1, keepdims=True)
    spread = jnp.mean(center * center, axis=-1, keepdims=True)
    scale = lax.rsqrt(spread + epsilon)
    normed = center * scale
    return (normed * gain + shift, normed, scale)


def norm_back(grad_out, normed, scale, gain):
    grad_norm = grad_out * gain
    grad_in = scale * (
        grad_norm
        - jnp.mean(grad_norm, axis=-1, keepdims=True)
        - normed * jnp.mean(grad_norm * normed, axis=-1, keepdims=True)
    )
    return (grad_in, jnp.sum(grad_out * normed, axis=0), jnp.sum(grad_out, axis=0))


def run_copies(copies, sems):
    started = [pltpu.make_async_copy(a, b, sems.at[i]) for i, (a, b) in enumerate(copies)]
    for copy in started:
        copy.start()
    for copy in started:
        copy.wait()


def pack_rows(parts):
    counts = [part.shape[0] for part in parts]
    width = parts[0].shape[1]

    def kernel(*refs):
        ins, out, sems = refs[: len(parts)], refs[-2], refs[-1]
        copies = []
        start = 0
        for ref, count in zip(ins, counts):
            copies.append((ref, out.at[pl.ds(start, count)]))
            start += count
        run_copies(copies, sems)

    return pl.pallas_call(
        kernel,
        out_shape=jax.ShapeDtypeStruct((sum(counts), width), parts[0].dtype),
        in_specs=[ANY] * len(parts),
        out_specs=INSIDE,
        scratch_shapes=[pltpu.SemaphoreType.DMA((len(parts),))],
    )(*parts)


def assemble(pieces, counts):
    arrays = [piece[0] for piece in pieces]
    width = arrays[0].shape[1]

    def kernel(*refs):
        ins, outs, sems = refs[: len(arrays)], refs[len(arrays) : -1], refs[-1]
        me = lax.axis_index("grp")
        low = lax.axis_index("rep") & 1
        copies = []
        for ref, (_, step, half) in zip(ins, pieces):
            start = 0
            for out, count in zip(outs, counts):
                rows = count if half is None else count // 2
                at = (me ^ step) * count
                if half is not None:
                    at = at + (low ^ half) * rows
                copies.append((ref.at[pl.ds(start, rows)], out.at[pl.ds(pl.multiple_of(at, 32), rows)]))
                start += rows
        run_copies(copies, sems)

    return pl.pallas_call(
        kernel,
        out_shape=[jax.ShapeDtypeStruct((4 * count, width), arrays[0].dtype) for count in counts],
        in_specs=[ANY] * len(arrays),
        out_specs=[INSIDE] * len(counts),
        scratch_shapes=[pltpu.SemaphoreType.DMA((len(arrays) * len(counts),))],
    )(*arrays)


def blocks_of(ref, side, core, width):
    if len(ref.shape) == 2:
        return [ref]
    return [ref.at[side, core, :, pl.ds(k, width)] for k in range(0, ref.shape[3], width)]


def height(part, width):
    return part.shape[-2] * (part.shape[-1] // width)


def stack_rows(vectors, rows, width):
    def kernel(*refs):
        out, held = refs[-2:]
        held[...] = jnp.zeros_like(held)
        line = 0
        for ref in refs[:-2]:
            for k in range(ref.shape[0] // width):
                held[line, :] = ref[pl.ds(k * width, width)]
                line += 1
        out[...] = held[...].astype(LOW)

    return pl.pallas_call(
        kernel,
        out_shape=jax.ShapeDtypeStruct((rows, width), LOW),
        in_specs=[INSIDE] * len(vectors),
        out_specs=INSIDE,
        scratch_shapes=[pltpu.VMEM((rows, width), F32)],
    )(*vectors)


def send_rows(parts, width):
    def kernel(*refs):
        ins, out, sems = refs[: len(parts)], refs[-2], refs[-1]
        other = 1 - (lax.axis_index("grp") & 1)
        copies = []
        for far in range(2):
            start = 0
            for ref in ins:
                for block in blocks_of(ref, far, other, width):
                    copies.append((block, out.at[far, pl.ds(start, block.shape[0])]))
                    start += block.shape[0]
        run_copies(copies, sems)

    return pl.pallas_call(
        kernel,
        out_shape=jax.ShapeDtypeStruct((2, sum(height(part, width) for part in parts), width), parts[0].dtype),
        in_specs=[ANY] * len(parts),
        out_specs=INSIDE,
        scratch_shapes=[pltpu.SemaphoreType.DMA((64,))],
    )(*parts)


def halve_first(parts, got, cuts):
    total, width = got.shape[1:]

    def kernel(*refs):
        ins, outs = refs[: len(parts) + 1], refs[len(parts) + 1 : -3]
        own, come, sems = refs[-3:]
        me = lax.axis_index("grp")
        core, far = me & 1, me >> 1
        copies = [(ins[-1], come)]
        for side in range(2):
            start = 0
            for ref in ins[:-1]:
                for block in blocks_of(ref, side, core, width):
                    copies.append((block, own.at[side, pl.ds(start, block.shape[0])]))
                    start += block.shape[0]
        run_copies(copies, sems)
        start = 0
        for k, count in enumerate(cuts):
            rows = pl.ds(start, count)
            for out, side in ((outs[2 * k], 1 - far), (outs[2 * k + 1], far)):
                out[...] = (own[side, rows].astype(F32) + come[side, rows].astype(F32)).astype(LOW)
            start += count

    return pl.pallas_call(
        kernel,
        out_shape=[jax.ShapeDtypeStruct((count, width), LOW) for count in cuts for _ in range(2)],
        in_specs=[ANY] * (len(parts) + 1),
        out_specs=[INSIDE] * (2 * len(cuts)),
        scratch_shapes=[pltpu.VMEM((2, total, width), LOW)] * 2 + [pltpu.SemaphoreType.DMA((64,))],
    )(*parts, got)


def halve(kept, got, step):
    kept, got = [part.reshape((2, part.shape[0] // 2) + part.shape[1:]) for part in (kept, got)]

    def kernel(kept_ref, got_ref, sent, rest):
        side = (lax.axis_index("rep") // step) & 1
        sent[...] = (kept_ref[1 - side].astype(F32) + got_ref[1 - side].astype(F32)).astype(LOW)
        rest[...] = (kept_ref[side].astype(F32) + got_ref[side].astype(F32)).astype(LOW)

    shape = jax.ShapeDtypeStruct(kept.shape[1:], LOW)
    return pl.pallas_call(
        kernel, out_shape=[shape, shape], in_specs=[INSIDE, INSIDE], out_specs=[INSIDE, INSIDE]
    )(kept, got)


def add_low(kept, got):
    def kernel(kept_ref, got_ref, out):
        out[...] = (kept_ref[...].astype(F32) + got_ref[...].astype(F32)).astype(LOW)

    return pl.pallas_call(
        kernel, out_shape=jax.ShapeDtypeStruct(kept.shape, LOW), in_specs=[INSIDE, INSIDE], out_specs=INSIDE
    )(kept, got)


def join(mine, other, step, dtype):
    def kernel(mine_ref, other_ref, out):
        side = (lax.axis_index("rep") // step) & 1
        out[side] = mine_ref[...].astype(dtype)
        out[1 - side] = other_ref[...].astype(dtype)

    both = pl.pallas_call(
        kernel,
        out_shape=jax.ShapeDtypeStruct((2,) + mine.shape, dtype),
        in_specs=[INSIDE, INSIDE],
        out_specs=INSIDE,
    )(mine, other)
    return both.reshape((2 * mine.shape[0],) + mine.shape[1:])


def spread(mine, other, items, shapes, sizes=()):
    half, width = mine.shape
    lines = sum(4 * size // width for size in sizes)
    first_line = sum(count for _, _, count in items)

    def kernel(mine_ref, other_ref, *outs):
        side = lax.axis_index("rep") & 1
        group = lax.axis_index("grp")
        arrays, vectors = outs[: len(shapes)], outs[len(shapes) :]
        for low in range(2):

            @pl.when(side == low)
            def _():
                start = 0
                for index, column, count in items:
                    for k in range(2):
                        first, last = max(start, k * half), min(start + count, (k + 1) * half)
                        if first < last:
                            ref = mine_ref if k == low else other_ref
                            rows = ref[pl.ds(first - k * half, last - first)].astype(F32)
                            arrays[index][pl.ds(first - start, last - first), pl.ds(column, width)] = rows
                    start += count
                if lines:
                    ref = mine_ref if low == 1 else other_ref
                    block = ref[pl.ds(first_line - half, 16)].astype(F32)
                    for owner in range(4):

                        @pl.when(group == owner)
                        def _():
                            line = 0
                            for out, size in zip(vectors, sizes):
                                at = owner * size
                                row, lane = line + at // width, at % width
                                out[...] = block[row, lane : lane + size]
                                line += 4 * size // width

    return pl.pallas_call(
        kernel,
        out_shape=[jax.ShapeDtypeStruct(shape, F32) for shape in shapes] + [jax.ShapeDtypeStruct((size,), F32) for size in sizes],
        in_specs=[INSIDE, INSIDE],
        out_specs=[INSIDE] * (len(shapes) + len(sizes)),
    )(mine, other)


def nt_dot(left, right):
    return lax.dot_general(left, right, (((1,), (1,)), ((), ())), preferred_element_type=F32)


def nn_dot(left, right):
    return lax.dot_general(left, right, (((1,), (0,)), ((), ())), preferred_element_type=F32)


def attend(place, queries, keys, values, prev_logits):
    rows, width = queries.shape
    length = keys.shape[0]
    head_dim = width // HEADS
    each = 128 // head_dim
    cols = each * head_dim

    def kernel(place_ref, q_ref, k_ref, v_ref, prev_ref, new_ref, prob_ref, ctx_ref):
        lane = lax.broadcasted_iota(jnp.int32, (rows, cols), 1)
        key_pos = lax.broadcasted_iota(jnp.int32, (rows, length), 1)
        query_pos = place_ref[1] + lax.broadcasted_iota(jnp.int32, (rows, length), 0)
        allowed = (key_pos < place_ref[0]) | (key_pos <= query_pos)
        q = q_ref[...].astype(F32) * 0.125
        k = k_ref[...]
        v = v_ref[...]
        context = jnp.zeros((rows, cols), F32)
        for h in range(each):
            mine = (lane >= h * head_dim) & (lane < (h + 1) * head_dim)
            scores = nt_dot(jnp.where(mine, q, 0.0).astype(LOW), k) + prev_ref[h].astype(F32)
            new_ref[h] = scores.astype(LOW)
            scores = jnp.where(allowed, scores, -1e30)
            terms = jnp.exp(scores - jnp.max(scores, axis=-1, keepdims=True))
            probs = (terms * (1.0 / jnp.sum(terms, axis=-1, keepdims=True))).astype(LOW)
            prob_ref[h] = probs
            context = jnp.where(mine, nn_dot(probs, v), context)
        ctx_ref[...] = context.astype(LOW)

    tall = pl.BlockSpec((length, cols), lambda i: (0, i))
    wide = pl.BlockSpec((rows, cols), lambda i: (0, i))
    square = pl.BlockSpec((each, rows, length), lambda i: (i, 0, 0))
    squares = jax.ShapeDtypeStruct((HEADS, rows, length), LOW)
    return pl.pallas_call(
        kernel,
        grid=(HEADS // each,),
        out_shape=[squares, squares, jax.ShapeDtypeStruct((rows, width), LOW)],
        in_specs=[pl.BlockSpec(memory_space=pltpu.SMEM), wide, tall, tall, square],
        out_specs=[square, square, wide],
    )(place, queries, keys, values, prev_logits)


def attend_back(queries, keys, values, probs, logit_grad, grad_context):
    rows, width = queries.shape
    length = keys.shape[0]
    head_dim = width // HEADS
    each = 128 // head_dim
    cols = each * head_dim

    def kernel(q_ref, k_ref, v_ref, prob_ref, lg_ref, dc_ref, ds_ref, dq_ref, dk_ref, dv_ref):
        lane = lax.broadcasted_iota(jnp.int32, (rows, cols), 1)
        dc = dc_ref[...].astype(F32)
        dc_turned = dc.T.astype(LOW)
        q_turned = (q_ref[...].astype(F32) * 0.125).T.astype(LOW)
        k = k_ref[...]
        v = v_ref[...]
        dq = jnp.zeros((rows, cols), F32)
        dk, dv = [], []
        for h in range(each):
            own = slice(h * head_dim, (h + 1) * head_dim)
            mine = (lane >= h * head_dim) & (lane < (h + 1) * head_dim)
            prob_low = prob_ref[h]
            prob = prob_low.astype(F32)
            dp = nt_dot(jnp.where(mine, dc, 0.0).astype(LOW), v)
            ds = prob * (dp - jnp.sum(dp * prob, axis=-1, keepdims=True)) + lg_ref[h].astype(F32)
            ds = ds.astype(LOW)
            ds_ref[h] = ds
            dq = jnp.where(mine, nn_dot(ds, k), dq)
            dv.append(nn_dot(dc_turned[own], prob_low))
            dk.append(nn_dot(q_turned[own], ds))
        dq_ref[...] = (dq * 0.125).astype(LOW)
        dk_ref[...] = jnp.concatenate(dk, axis=0).T.astype(LOW)
        dv_ref[...] = jnp.concatenate(dv, axis=0).T.astype(LOW)

    tall = pl.BlockSpec((length, cols), lambda i: (0, i))
    wide = pl.BlockSpec((rows, cols), lambda i: (0, i))
    square = pl.BlockSpec((each, rows, length), lambda i: (i, 0, 0))
    talls = jax.ShapeDtypeStruct((length, width), LOW)
    return pl.pallas_call(
        kernel,
        grid=(HEADS // each,),
        out_shape=[jax.ShapeDtypeStruct((HEADS, rows, length), LOW), jax.ShapeDtypeStruct((rows, width), LOW), talls, talls],
        in_specs=[wide, tall, tall, square, square, wide],
        out_specs=[square, wide, tall, tall],
    )(queries, keys, values, probs, logit_grad, grad_context)


def make_body(rep_size, grp_size):
    def swap(value, axis, bit):
        size = rep_size if axis == "rep" else grp_size
        return lax.ppermute(value, axis, [(i, i ^ bit) for i in range(size)])

    def pick(value, index, axis=0):
        return lax.dynamic_index_in_dim(value, index, axis, keepdims=False)

    def gather_group(shard):
        far = swap(shard, "grp", 2)
        near = swap(shard, "grp", 1)
        diag = swap(far, "grp", 1)
        return (shard, 0, None), (near, 1, None), (far, 2, None), (diag, 3, None)

    def gather_halves(shard, low):
        half = pick(in_two(shard), low)
        near = swap(shard, "grp", 1)
        far = swap(half, "grp", 2)
        side = swap(far, "rep", 1)
        diag = swap(far, "grp", 1)
        last = swap(side, "grp", 1)
        return (shard, 0, None), (near, 1, None), (far, 2, 0), (side, 2, 1), (diag, 3, 0), (last, 3, 1)

    def rep_bits(rep):
        count = rep_size.bit_length() - 1
        return [(1 << k, (rep >> k) & 1) for k in range(count)]

    def in_two(part):
        return part.reshape((2, part.shape[0] // 2) + part.shape[1:])

    def reduce_group(values, width, cuts=None, shared=()):
        split = [value.reshape((2, 2, value.shape[0] // 4) + value.shape[1:]) for value in values] + list(shared)
        got = swap(send_rows(split, width), "grp", 1)
        halves = halve_first(split, got, cuts or (got.shape[1],))
        return halves[1], swap(halves[0], "grp", 2), *halves[2:]

    def reduce_rep(kept, got, bits):
        for step, _ in bits[:-1]:
            sent, kept = halve(kept, got, step)
            got = swap(sent, "rep", step)
        value = add_low(kept, got)
        step = bits[-1][0]
        value = add_low(value, swap(value, "rep", step))
        for step, _ in reversed(bits[1:-1]):
            value = join(value, swap(value, "rep", step), step, LOW)
        return value, swap(value, "rep", 1)

    def inner_body(
        hidden,
        prev_logits,
        prefix,
        w_query,
        w_key,
        w_value,
        w_output,
        w_inner,
        w_outer,
        b_query,
        b_value,
        b_output,
        b_inner,
        b_outer,
        gain_attn,
        shift_attn,
        gain_feed,
        shift_feed,
        out_grad,
        logit_grad,
    ):
        rows, width = hidden.shape
        shard = w_query.shape[0]
        hidden_width = w_inner.shape[1]
        feed_shard = w_outer.shape[0]
        rep = lax.axis_index("rep")
        group = lax.axis_index("grp")
        bits = rep_bits(rep)
        pack = pack_rows((hidden, w_query, w_key, w_value))
        pack_pieces = gather_group(pack)
        vectors = (b_query, b_value, b_output, b_inner, b_outer, gain_attn, shift_attn, gain_feed, shift_feed)
        vec_sizes = [item.shape[0] for item in vectors]
        vec_count = sum(vec_sizes)
        vec = jnp.concatenate(vectors)
        vec_pieces = gather_group(vec)
        output_pieces = gather_group(w_output)
        inner_pieces = gather_halves(w_inner, rep & 1)
        outer_pieces = gather_halves(w_outer, rep & 1)

        vec_all = jnp.zeros((4, vec_count), F32)
        for piece, step, _ in vec_pieces:
            vec_all = lax.dynamic_update_index_in_dim(vec_all, piece.astype(F32), group ^ step, 0)
        full_vectors = []
        offset = 0
        for size in vec_sizes:
            full_vectors.append(vec_all[:, offset : offset + size].reshape(4 * size))
            offset += size
        query_bias, value_bias, output_bias, inner_bias, outer_bias = full_vectors[:5]
        attn_gain, attn_shift, feed_gain, feed_shift = full_vectors[5:]

        tokens_all, query_mat, key_mat, value_mat = assemble(pack_pieces, (rows, shard, shard, shard))
        queries = (mat_dot(hidden, query_mat) + query_bias).astype(LOW)
        group_keys = mat_dot(tokens_all, key_mat).astype(LOW)
        group_values = (mat_dot(tokens_all, value_mat) + value_bias).astype(LOW)
        position = jnp.stack([prefix[rep], (group * rows).astype(jnp.int32)])
        new_logits, probs, context = attend(position, queries, group_keys, group_values, prev_logits)
        (output_mat,) = assemble(output_pieces, (shard,))
        (inner_mat,) = assemble(inner_pieces, (shard,))
        (outer_mat,) = assemble(outer_pieces, (feed_shard,))

        attn_out = mat_dot(context, output_mat) + output_bias
        first_out, first_norm, first_scale = layer_norm(hidden.astype(F32) + attn_out, attn_gain, attn_shift)
        first_low = first_out.astype(LOW)
        inner_act = mat_dot(first_low, inner_mat) + inner_bias
        gelu_out, gelu_pull = jax.vjp(jax.nn.gelu, inner_act)
        middle, slope = gelu_out.astype(LOW), gelu_pull(jnp.ones_like(inner_act))[0]
        middle, slope = lax.optimization_barrier((middle, slope))
        feed_out = mat_dot(middle, outer_mat) + outer_bias
        output, second_norm, second_scale = layer_norm(first_low.astype(F32) + feed_out, feed_gain, feed_shift)
        grad_second, grad_gfeed, grad_sfeed = norm_back(
            out_grad.astype(F32), second_norm, second_scale, feed_gain
        )
        grad_feed = lax.optimization_barrier(grad_second.astype(LOW))
        grad_bouter = jnp.sum(grad_feed.astype(F32), axis=0)
        grad_wouter = left_dot(middle, grad_feed).astype(LOW)
        outer_pair = reduce_rep(*reduce_group([grad_wouter], width), bits)
        grad_inner = (right_dot(grad_feed, outer_mat) * slope).astype(LOW)
        grad_inner = lax.optimization_barrier(grad_inner)
        grad_binner = jnp.sum(grad_inner.astype(F32), axis=0)
        grad_winner = left_dot(first_low, grad_inner).astype(LOW)
        grad_first = grad_second + right_dot(grad_inner, inner_mat)
        grad_resid, grad_gattn, grad_sattn = norm_back(grad_first, first_norm, first_scale, attn_gain)
        grad_attn = lax.optimization_barrier(grad_resid.astype(LOW))
        grad_boutput = jnp.sum(grad_attn.astype(F32), axis=0)
        grad_context = right_dot(grad_attn, output_mat).astype(LOW)
        grad_woutput = left_dot(context, grad_attn).astype(LOW)
        inner_pair = reduce_rep(*reduce_group([grad_winner, grad_woutput], width), bits)
        grad_scores, grad_queries, grad_keys, grad_values = attend_back(
            queries, group_keys, group_values, probs, logit_grad, grad_context
        )
        grad_bquery = jnp.sum(grad_queries.astype(F32), axis=0)
        grad_bvalue = jnp.sum(grad_values.astype(F32), axis=0)
        grad_wquery = left_dot(hidden, grad_queries)
        grad_wkey = left_dot(tokens_all, grad_keys)
        grad_wvalue = left_dot(tokens_all, grad_values)
        grad_rows = (right_dot(grad_keys, key_mat) + right_dot(grad_values, value_mat)).astype(LOW)

        grad_own = grad_resid + right_dot(grad_queries, query_mat)

        vec_grads = (
            grad_bquery,
            grad_bvalue,
            grad_boutput,
            grad_binner,
            grad_bouter,
            grad_gattn,
            grad_sattn,
            grad_gfeed,
            grad_sfeed,
        )
        vec_rows = 32
        vec_value = stack_rows(vec_grads, vec_rows, width)
        attn_values = [item.astype(LOW) for item in (grad_rows, grad_wquery, grad_wkey, grad_wvalue)]
        cuts = (rows, 3 * shard + vec_rows)
        rows_kept, rows_got, sent, kept = reduce_group(attn_values, width, cuts, (vec_value,))
        grad_input = grad_own + rows_kept.astype(F32) + rows_got.astype(F32)
        got = swap(sent, "grp", 2)
        square = (shard, width)
        attn_pair = reduce_rep(kept, got, bits)
        outs = spread(*attn_pair, [(k, 0, shard) for k in range(3)], [square] * 3, vec_sizes)
        attn_grads, vec_outs = outs[:3], outs[3:]
        items = [(0, k, shard) for k in range(0, hidden_width, width)] + [(1, 0, shard)]
        grad_winner, grad_woutput = spread(*inner_pair, items, [(shard, hidden_width), square])
        return (
            output.astype(LOW),
            new_logits,
            grad_input.astype(LOW),
            grad_scores,
            *attn_grads,
            grad_woutput,
            grad_winner,
            join(*outer_pair, 1, F32),
            *vec_outs,
        )

    return inner_body


def solution(mesh):
    rows = P(("rep", "grp"), None)
    logits = P(None, ("rep", "grp"), None)
    matrix = P("grp", None)
    vector = P("grp")
    return jax.shard_map(
        make_body(mesh.shape["rep"], mesh.shape["grp"]),
        mesh=mesh,
        in_specs=(rows, logits, P(), *(matrix,) * 6, *(vector,) * 9, rows, logits),
        out_specs=(rows, logits, rows, logits, *(matrix,) * 6, *(vector,) * 9),
        check_vma=False,
    )
```
